32 devices in a mesh: rep: 8 (over y, x, core), seq: 4 (over z).
Axes of the slice: x: 2, y: 2, z: 4, core: 2. Of those that a mesh axis runs over, the one named last changes fastest.
Arguments:
- tokens: bfloat16 [16384, 896], P(('rep', 'seq')), may hold values from -6 to 6
- cotangent: bfloat16 [16384, 896], P(('rep', 'seq')), may hold values from -6 to 6
- seq_ids: int32 [16384], P(('rep', 'seq')), may hold values from 0 to 4, as said below
- block_ids: int32 [16384], P(('rep', 'seq')), may hold values from 0 to 3, as said below
- positions: int32 [16384], P(('rep', 'seq')), may hold values from 0 to 1023, as said below
- first_gain: bfloat16 [896], P('seq'), may hold values from 0.5 to 1.5
- query_weight: bfloat16 [896, 896], P('seq'), may hold values from -0.1875 to 0.1875
- query_bias: bfloat16 [896], P('seq'), may hold values from -1.796875 to 1.796875
- key_weight: bfloat16 [896, 128], P('seq'), may hold values from -0.1875 to 0.1875
- key_bias: bfloat16 [128], P('seq'), may hold values from -1.796875 to 1.796875
- value_weight: bfloat16 [896, 128], P('seq'), may hold values from -0.1875 to 0.1875
- value_bias: bfloat16 [128], P('seq'), may hold values from -0.119628906 to 0.119628906
- out_weight: bfloat16 [896, 896], P('seq'), may hold values from -2 to 2
- second_gain: bfloat16 [896], P('seq'), may hold values from 0.5 to 1.5
- gate_weight: bfloat16 [896, 4864], P('seq'), may hold values from -0.1875 to 0.1875
- up_weight: bfloat16 [896, 4864], P('seq'), may hold values from -0.1875 to 0.1875
- down_weight: bfloat16 [4864, 896], P('seq'), may hold values from -0.078125 to 0.078125
Outputs:
- output: bfloat16 [16384, 896], P(('rep', 'seq'))
- tokens_grad: bfloat16 [16384, 896], P(('rep', 'seq'))
- first_gain_grad: float32 [896], P('seq')
- query_weight_grad: float32 [896, 896], P('seq')
- query_bias_grad: float32 [896], P('seq')
- key_weight_grad: float32 [896, 128], P('seq')
- key_bias_grad: float32 [128], P('seq')
- value_weight_grad: float32 [896, 128], P('seq')
- value_bias_grad: float32 [128], P('seq')
- out_weight_grad: float32 [896, 896], P('seq')
- second_gain_grad: float32 [896], P('seq')
- gate_weight_grad: float32 [896, 4864], P('seq')
- up_weight_grad: float32 [896, 4864], P('seq')
- down_weight_grad: float32 [4864, 896], P('seq')
The draws below stay inside these ranges and needn't reach their ends.
Inputs may be any that keep to these rules, and one draw needn't show every extreme that they name: `seq_ids`: each group of 2048 consecutive tokens holds whole sequences made of whole blocks of 256 tokens, numbered 0, 1, 2, ... in order within the group; a sequence has 1 to 4 blocks, and each group has one of exactly 4 blocks, which begins at the last block of some run of 2 blocks (block index k * 2 - 1 within the group); the largest number, 4, is reached in some group. `block_ids`: the index of the token's block of 256 tokens within its sequence. The token's index within its sequence, so that positions // 256 equals block_ids.
All inputs are finite; a program needn't handle non-finite values.
Results may differ from the reference program's by a relative error of at most 0.024.
Values may be sent and summed in bfloat16 or wider, within the bound.
No kernel may reach another device: no remote copies, remote signals or barrier semaphores. Data moves between devices by JAX's collectives and lax.ppermute only.
A program may use at most 256 MiB of HBM per device.

```python
import jax
import jax.numpy as jnp
from jax import lax

D = 896
H = 14
KVH = 2
HD = 64
FF = 4864
BLK = 256
SEQ_BLOCKS = 4
BLK_DEV = 2
KV = 128
GROUP_BLOCKS = 8
GROUP_TOK = 2048
GROUPS = 8
TOKENS = 16384


def layout_parts(key):
    base_key = jax.random.fold_in(key, 11)
    group_keys = jax.random.split(base_key, GROUPS)
    group_index_all = jnp.arange(GROUPS, dtype=jnp.int32)
    start_count = (GROUP_BLOCKS - SEQ_BLOCKS - BLK_DEV + 1) // BLK_DEV + 1

    def one_group(group_key, group_index):
        first_key, second_key = jax.random.split(group_key)
        first_block = BLK_DEV - 1 + BLK_DEV * jax.random.randint(first_key, (), 0, start_count)
        coin_flips = jax.random.randint(second_key, (GROUP_BLOCKS,), 0, 2)
        coin_flips = jnp.where(group_index == 0, 1, coin_flips)
        block_index = jnp.arange(GROUP_BLOCKS, dtype=jnp.int32)
        inside = (block_index >= first_block) & (block_index < first_block + SEQ_BLOCKS)
        offset = jnp.where(block_index < first_block, block_index, block_index - first_block - SEQ_BLOCKS)
        outside_flag = jnp.where(offset % 2 == 0, 1, coin_flips)
        new_flags = jnp.where(inside, jnp.where(block_index == first_block, 1, 0), outside_flag)
        seq_block = jnp.cumsum(new_flags) - 1
        seq_starts = lax.cummax(jnp.where(new_flags == 1, block_index, 0), axis=0)
        within = block_index - seq_starts
        seq_tok = jnp.repeat(seq_block, BLK)
        block_tok = jnp.repeat(within, BLK)
        place_tok = block_tok * BLK + jnp.tile(jnp.arange(BLK, dtype=jnp.int32), GROUP_BLOCKS)
        return (seq_tok, block_tok, place_tok)
    seq_all, block_all, place_all = jax.vmap(one_group)(group_keys, group_index_all)
    return (seq_all.reshape(TOKENS).astype(jnp.int32), block_all.reshape(TOKENS).astype(jnp.int32), place_all.reshape(TOKENS).astype(jnp.int32))


def draw_seq_ids(key, part):
    return layout_parts(key)[0]


def draw_block_ids(key, part):
    return layout_parts(key)[1]


def draw_positions(key, part):
    return layout_parts(key)[2]


def block_levels(rng, dims, shards, low, largest):
    loudness = 1.0
    for axis_at, blocks in shards:
        draws = jax.random.uniform(jax.random.fold_in(jax.random.fold_in(rng, 6), axis_at), (blocks,), jnp.float32, low / len(shards), largest / len(shards))
        loudness = loudness * jnp.repeat(jnp.exp(draws), dims[axis_at] // blocks).reshape((-1,) + (1,) * (len(dims) - 1 - axis_at))
    return loudness


def scatter_about(key, shape, deviation, reach, shards=(), kind=jnp.bfloat16):
    values = jax.random.normal(key, shape, jnp.float32) * deviation
    if len(shards) > 0:
        values = block_levels(key, shape, shards, -0.22, 0.18) * values
    return jnp.clip(values, min=-reach, max=reach).astype(kind)


def setup_inputs(seed: int = 0) -> dict:
    arg_keys = jax.random.split(jax.random.key(seed), 18)
    tokens = scatter_about(arg_keys[0], (TOKENS, D), 1.0, 6.0, ((0, 32),))
    cotangent = scatter_about(arg_keys[1], (TOKENS, D), 1.0, 6.0, ((0, 32),))
    seq_ids = draw_seq_ids(jax.random.fold_in(arg_keys[17], 71), 0)
    block_ids = draw_block_ids(jax.random.fold_in(arg_keys[17], 71), 0)
    positions = draw_positions(jax.random.fold_in(arg_keys[17], 71), 0)
    first_gain = jnp.clip(1.0 + 0.1 * jax.random.normal(arg_keys[5], (D,), jnp.float32), 0.5, 1.5).astype(jnp.bfloat16)
    query_weight = scatter_about(arg_keys[6], (D, D), D ** -0.5, 0.1875, ((0, 4),))
    query_bias = scatter_about(arg_keys[7], (D,), 0.3, 1.796875, ((0, 4),))
    key_weight = scatter_about(arg_keys[8], (D, KV), D ** -0.5, 0.1875, ((0, 4),))
    key_bias = scatter_about(arg_keys[9], (KV,), 0.3, 1.796875, ((0, 4),))
    value_weight = scatter_about(arg_keys[10], (D, KV), D ** -0.5, 0.1875, ((0, 4),))
    value_bias = scatter_about(arg_keys[11], (KV,), 0.02, 0.119628906, ((0, 4),))
    out_weight = scatter_about(arg_keys[12], (D, D), (max(D // 128, 1)) ** -0.5, 2.0, ((0, 4),))
    second_gain = jnp.clip(1.0 + 0.1 * jax.random.normal(arg_keys[13], (D,), jnp.float32), 0.5, 1.5).astype(jnp.bfloat16)
    gate_weight = scatter_about(arg_keys[14], (D, FF), D ** -0.5, 0.1875, ((0, 4),))
    up_weight = scatter_about(arg_keys[15], (D, FF), D ** -0.5, 0.1875, ((0, 4),))
    down_weight = scatter_about(arg_keys[16], (FF, D), FF ** -0.5, 0.078125, ((0, 4),))
    return dict(tokens=tokens, cotangent=cotangent, seq_ids=seq_ids, block_ids=block_ids, positions=positions, first_gain=first_gain, query_weight=query_weight, query_bias=query_bias, key_weight=key_weight, key_bias=key_bias, value_weight=value_weight, value_bias=value_bias, out_weight=out_weight, second_gain=second_gain, gate_weight=gate_weight, up_weight=up_weight, down_weight=down_weight)


EPS = 1e-06
ROPE_BASE = 1000000.0
NEG_FILL = -1e+30

@jax.custom_vjp
def low(v):
    return lax.optimization_barrier(v.astype(jnp.bfloat16)).astype(jnp.float32)

@jax.custom_vjp
def low_back(v):
    return v

def low_keep(v):
    return (low(v), None)

def low_pass(kept, grad):
    return (grad,)

def back_keep(v):
    return (v, None)

def back_low(kept, grad):
    return (low(grad),)
low.defvjp(low_keep, low_pass)
low_back.defvjp(back_keep, back_low)

def matmul(left, right):
    return jnp.dot(left, right, precision=lax.Precision.HIGHEST, preferred_element_type=jnp.float32)

def rope_tables(positions):
    half_size = HD // 2
    freqs = ROPE_BASE ** (-(jnp.arange(half_size, dtype=jnp.float32) * 2.0 / HD))
    angles = positions.astype(jnp.float32)[:, None] * freqs[None, :]
    angles = jnp.concatenate([angles, angles], axis=-1)
    return (jnp.cos(angles), jnp.sin(angles))

def rotate(values, cosine, sine_table):
    half_size = values.shape[-1] // 2
    turned = jnp.concatenate([-values[..., half_size:], values[..., :half_size]], axis=-1)
    return values * cosine[:, None, :] + turned * sine_table[:, None, :]

def head_attention(query_head, key_head, value_head, allowed):
    scores = low_back(matmul(query_head, key_head.T) * HD ** (-0.5))
    scores = jnp.where(allowed, scores, NEG_FILL)
    top_score = lax.optimization_barrier(jnp.max(scores, axis=-1, keepdims=True))
    expon = jnp.exp(scores - top_score)
    probs = expon / lax.optimization_barrier(jnp.sum(expon, axis=-1, keepdims=True))
    return matmul(low(probs), value_head)

def forward(weights, tokens_in, cosine, sine_table, allowed):
    gain_one, w_query, b_query, w_key, b_key, w_value, b_value, w_out, gain_two, w_gate, w_up, w_down = weights
    row_count = tokens_in.shape[0]
    scale_one = lax.rsqrt(lax.optimization_barrier(jnp.mean(tokens_in * tokens_in, axis=-1, keepdims=True)) + EPS)
    normed = low(tokens_in * scale_one * gain_one)
    query_pre = low_back(matmul(normed, w_query) + b_query)
    key_pre = low_back(matmul(normed, w_key) + b_key)
    value_rows = low(low_back(matmul(normed, w_value) + b_value))
    queries = low(rotate(query_pre.reshape(row_count, H, HD), cosine, sine_table))
    key_rows = low(rotate(key_pre.reshape(row_count, KVH, HD), cosine, sine_table))
    value_rows = value_rows.reshape(row_count, KVH, HD)
    group_heads = H // KVH
    query_heads = jnp.transpose(queries, (1, 0, 2))
    key_heads = jnp.repeat(jnp.transpose(key_rows, (1, 0, 2)), group_heads, axis=0)
    value_heads = jnp.repeat(jnp.transpose(value_rows, (1, 0, 2)), group_heads, axis=0)

    def one_head(triple):
        return head_attention(triple[0], triple[1], triple[2], allowed)
    attended = lax.map(jax.checkpoint(one_head), (query_heads, key_heads, value_heads))
    attended = jnp.transpose(attended, (1, 0, 2)).reshape(row_count, H * HD)
    attended = low(low_back(attended))
    mixed = tokens_in + low_back(matmul(attended, w_out))
    scale_two = lax.rsqrt(lax.optimization_barrier(jnp.mean(mixed * mixed, axis=-1, keepdims=True)) + EPS)
    normed_two = low(mixed * scale_two * gain_two)
    gate = low_back(matmul(normed_two, w_gate))
    up_part = low_back(matmul(normed_two, w_up))
    hidden = low(jax.nn.silu(gate) * up_part)
    return mixed + low_back(matmul(hidden, w_down))

def reference(tokens, cotangent, seq_ids, block_ids, positions, first_gain, query_weight, query_bias, key_weight, key_bias, value_weight, value_bias, out_weight, second_gain, gate_weight, up_weight, down_weight):
    weights = tuple((w_item.astype(jnp.float32) for w_item in (first_gain, query_weight, query_bias, key_weight, key_bias, value_weight, value_bias, out_weight, second_gain, gate_weight, up_weight, down_weight)))
    batches = (tokens.reshape(GROUPS, GROUP_TOK, D), cotangent.reshape(GROUPS, GROUP_TOK, D), seq_ids.reshape(GROUPS, GROUP_TOK), block_ids.reshape(GROUPS, GROUP_TOK), positions.reshape(GROUPS, GROUP_TOK))

    def per_group(totals, batch):
        group_tokens, group_cot, group_seq, group_block, group_pos = batch
        cosine, sine_table = rope_tables(group_pos)
        allowed = (group_seq[:, None] == group_seq[None, :]) & (group_block[None, :] <= group_block[:, None])

        def layer(weight_set, tokens_in):
            return forward(weight_set, tokens_in, cosine, sine_table, allowed)
        result, pullback = jax.vjp(layer, weights, group_tokens.astype(jnp.float32))
        weight_grads, input_grad = pullback(group_cot.astype(jnp.float32))
        totals = jax.tree.map(lambda acc, extra: acc + extra, totals, weight_grads)
        return (totals, (result.astype(jnp.bfloat16), input_grad.astype(jnp.bfloat16)))
    zeros = tuple((jnp.zeros(w_item.shape, jnp.float32) for w_item in weights))
    totals, (results, input_grads) = lax.scan(per_group, zeros, batches)
    return (results.reshape(TOKENS, D), input_grads.reshape(TOKENS, D), totals[0], totals[1], totals[2], totals[3], totals[4], totals[5], totals[6], totals[7], totals[8], totals[9], totals[10], totals[11])
```

```python
import jax
import jax.numpy as jnp
from jax import lax
from jax.experimental import pallas as pl
from jax.experimental.pallas import tpu as pltpu
from jax.sharding import PartitionSpec as P

H = 14
KVH = 2
HD = 64
BLK = 256
SEQ_BLOCKS = 4
LANES = 128

EPS = 1e-06
ROPE_BASE = 1000000.0

F32 = jnp.float32
BF16 = jnp.bfloat16


class Net:
    def __init__(self):
        self.reps = lax.axis_size("rep")
        self.seqs = lax.axis_size("seq")
        self.rep = lax.axis_index("rep").astype(jnp.int32)
        self.seq = lax.axis_index("seq").astype(jnp.int32)
        self.place = jnp.stack([self.rep, self.seq])
        self.pairs = self.reps // 2
        self.half = self.rep % 2
        self.pair = self.rep // 2
        bits = []
        bit = 1
        while bit < self.pairs:
            bits.append(bit)
            bit *= 2
        self.orders = (tuple(bits), tuple(bits[::-1]))
        self.same_half = [[2 * k + c for k in range(self.pairs)] for c in range(2)]

    def flip(self, value, bit):
        return lax.ppermute(value, "rep", [(i, i ^ bit) for i in range(self.reps)])

    def flip_seq(self, value, bit):
        return lax.ppermute(value, "seq", [(i, i ^ bit) for i in range(self.seqs)])

    def slide(self, value, step):
        pairs = [(i, i + step) for i in range(self.seqs) if 0 <= i + step < self.seqs]
        return lax.ppermute(value, "seq", pairs)

    def gather_seq(self, value):
        return lax.all_gather(value, "seq", axis=0, tiled=True)

    def spread(self, piece, order):
        held = {0: piece}
        for bit in order:
            held.update({m ^ bit: self.flip(v, 2 * bit) for m, v in list(held.items())})
        return [held[m] for m in range(self.pairs)]

    def grow(self, held, bit):
        held.update({m ^ bit: self.flip(v, 2 * bit) for m, v in list(held.items())})


class Fold:
    def __init__(self, net, parts, order):
        self.net = net
        self.keep, self.send = parts
        self.bits = list(order)

    def step(self):
        got = self.net.flip(self.send, 2 * self.bits.pop(0))
        half = self.keep.shape[0] // 2
        if half == 0:
            self.keep = (self.keep.astype(F32) + got.astype(F32)).astype(BF16)
            return
        self.send = (self.keep[half:].astype(F32) + got[half:].astype(F32)).astype(BF16)
        self.keep = (self.keep[:half].astype(F32) + got[:half].astype(F32)).astype(BF16)

    def state(self):
        return (self.keep, self.send) if self.bits else (self.keep,)

    def rest(self):
        while self.bits:
            self.step()
        return self.keep[0]


def after(value, *others):
    return lax.optimization_barrier((value, others))[0]


def cut_width(columns, parts):
    return pl.cdiv(columns // LANES, parts) * LANES


def cut_offset(index, columns, parts):
    width = cut_width(columns, parts)
    return jnp.minimum(index * width, columns - width)


def piece_of_rank(rank, order):
    count = len(order)
    piece = 0
    for at, bit in enumerate(order):
        piece = piece | (((rank >> (count - 1 - at)) & 1) * bit)
    return piece


def assemble(net, regions, columns, index, rows, steps, place_of, own=None):
    flat = [p for region in regions for p in region[3]]
    skip = 0 if own is None else 1

    def body(place, *refs):
        out = refs[-1]

        def fill():
            at = 0
            for start, span, parts, pieces in regions:
                for m, piece in enumerate(pieces):
                    offset = start + cut_offset(index(place) ^ m, span, parts)
                    col = pl.multiple_of(offset, LANES)
                    out[:, pl.ds(col, piece.shape[1])] = refs[at][...]
                    at += 1

        if own is None:
            fill()
        else:

            @pl.when(pl.program_id(0) == 0)
            def _():
                out[...] = refs[-2][...]

            @pl.when(pl.program_id(0) > 0)
            def _():
                fill()

    in_specs = [
        pl.BlockSpec((rows, p.shape[1]), lambda i, p: (jnp.maximum(i - skip, 0), 0)) for p in flat
    ]
    if own is not None:
        in_specs.append(pl.BlockSpec((rows, columns), lambda i, p: (0, 0)))
        flat = flat + [own]
    return pl.pallas_call(
        body,
        name="assemble",
        out_shape=jax.ShapeDtypeStruct((rows * steps, columns), flat[0].dtype),
        grid_spec=pltpu.PrefetchScalarGridSpec(
            num_scalar_prefetch=1,
            grid=(steps,),
            in_specs=in_specs,
            out_specs=pl.BlockSpec((rows, columns), lambda i, p: (place_of(i, p), 0)),
        ),
        cost_estimate=pl.CostEstimate(
            flops=0, transcendentals=0, bytes_accessed=4 * rows * steps * columns
        ),
    )(net.place, *flat)


def widen(stack, columns, moves, first, rows):
    count, _, width = stack.shape
    block = rows // 4
    skip = first // block

    def body(stack_ref, out_ref):
        for k, source, span, target in moves:
            out_ref[:, target : target + span] = stack_ref[k, :, source : source + span].astype(
                F32
            )

    return pl.pallas_call(
        body,
        name="widen",
        out_shape=jax.ShapeDtypeStruct((rows, columns), F32),
        grid=(4,),
        in_specs=[pl.BlockSpec((count, block, width), lambda i: (0, i + skip, 0))],
        out_specs=pl.BlockSpec((block, columns), lambda i: (i, 0)),
        cost_estimate=pl.CostEstimate(
            flops=0, transcendentals=0, bytes_accessed=6 * rows * columns
        ),
    )(stack)


def weight_grad(net, left_t, right, cuts, split_left):
    total, tokens = left_t.shape
    columns = right.shape[1]
    widths = [cut_width(span, net.pairs) for _, span, _ in cuts]
    half = net.pairs // 2
    shapes = [(w, columns) if split_left else (total, w) for w in widths]

    def body(place, left_ref, right_ref, *outs):
        step = pl.program_id(0)
        slabs = []
        for (start, span, order), width in zip(cuts, widths):
            piece = (place[0] // 2) ^ piece_of_rank(step, order)
            at = pl.multiple_of(start + cut_offset(piece, span, net.pairs), LANES)
            if split_left:
                slabs.append(left_ref[pl.ds(at, width), :])
            else:
                slabs.append(right_ref[:, pl.ds(at, width)])
        axis = 0 if split_left else 1
        slab = slabs[0] if len(slabs) == 1 else jnp.concatenate(slabs, axis=axis)
        pair = (slab, right_ref[...]) if split_left else (left_ref[...], slab)
        val = jnp.dot(*pair, preferred_element_type=F32).astype(BF16)

        def put(which):
            at = 0
            for k, width in enumerate(widths):
                span = slice(at, at + width)
                outs[2 * k + which][0] = val[span, :] if split_left else val[:, span]
                at += width

        @pl.when(step < half)
        def _():
            put(0)

        @pl.when(step >= half)
        def _():
            put(1)

    out_shape, out_specs = [], []
    for shape in shapes:
        out_shape += [jax.ShapeDtypeStruct((half,) + shape, BF16)] * 2
        out_specs += [
            pl.BlockSpec((1,) + shape, lambda i, p: (jnp.minimum(i, half - 1), 0, 0)),
            pl.BlockSpec((1,) + shape, lambda i, p: (jnp.maximum(i - half, 0), 0, 0)),
        ]
    outs = pl.pallas_call(
        body,
        name="weight_grad",
        out_shape=out_shape,
        grid_spec=pltpu.PrefetchScalarGridSpec(
            num_scalar_prefetch=1,
            grid=(net.pairs,),
            in_specs=[
                pl.BlockSpec((total, tokens), lambda i, p: (0, 0)),
                pl.BlockSpec((tokens, columns), lambda i, p: (0, 0)),
            ],
            out_specs=out_specs,
        ),
        cost_estimate=pl.CostEstimate(
            flops=2 * total * tokens * columns,
            transcendentals=0,
            bytes_accessed=2 * (total * tokens + tokens * columns + total * columns),
        ),
    )(net.place, left_t, right)
    return [tuple(outs[2 * k : 2 * k + 2]) for k in range(len(cuts))]


def attend_forward(queries_t, keys, values_t, runs):
    heads, size, rows = queries_t.shape
    total = keys.shape[1]
    blocks = rows // BLK
    lead = total // BLK - blocks

    def body(runs_ref, q_ref, k_ref, v_ref, o_ref):
        block = pl.program_id(0)
        run = runs_ref[block]
        for n in range(1, SEQ_BLOCKS + 1):

            @pl.when(run == n - 1)
            def _():
                low = pl.multiple_of((block + (lead + 1 - n)) * BLK, BLK)

                def head(h, carry):
                    g = h // (heads // KVH)
                    scores = jnp.dot(
                        k_ref[g, pl.ds(low, n * BLK), :], q_ref[h], preferred_element_type=F32
                    )
                    top = jnp.max(scores, axis=0, keepdims=True)
                    expon = jnp.exp(scores - top)
                    norm = jnp.sum(expon, axis=0, keepdims=True)
                    out = jnp.dot(
                        v_ref[g, :, pl.ds(low, n * BLK)],
                        expon.astype(BF16),
                        preferred_element_type=F32,
                    )
                    o_ref[h] = (out / norm).astype(BF16)
                    return carry

                lax.fori_loop(0, heads, head, 0, unroll=2)

    return pl.pallas_call(
        body,
        name="attend_forward",
        out_shape=jax.ShapeDtypeStruct((heads, size, rows), BF16),
        grid_spec=pltpu.PrefetchScalarGridSpec(
            num_scalar_prefetch=1,
            grid=(blocks,),
            in_specs=[
                pl.BlockSpec((heads, size, BLK), lambda i, r: (0, 0, i)),
                pl.BlockSpec((KVH, total, size), lambda i, r: (0, 0, 0)),
                pl.BlockSpec((KVH, size, total), lambda i, r: (0, 0, 0)),
            ],
            out_specs=pl.BlockSpec((heads, size, BLK), lambda i, r: (0, 0, i)),
        ),
        cost_estimate=pl.CostEstimate(
            flops=32 * heads * rows * total * size,
            transcendentals=heads * rows * total,
            bytes_accessed=8 * heads * rows * size,
        ),
    )(runs, queries_t, keys, values_t)


def attend_backward(queries_t, grads_t, keys, keys_t, values, runs):
    heads, size, rows = queries_t.shape
    total = keys.shape[1]
    blocks = rows // BLK
    lead = total // BLK - blocks

    def body(runs_ref, q_ref, g_ref, k_ref, kt_ref, v_ref, dq_ref, dk_ref, dv_ref, dk_acc, dv_acc):
        block = pl.program_id(0)
        run = runs_ref[block]

        @pl.when(block == 0)
        def _():
            dk_acc[...] = jnp.zeros_like(dk_acc)
            dv_acc[...] = jnp.zeros_like(dv_acc)

        for n in range(1, SEQ_BLOCKS + 1):

            @pl.when(run == n - 1)
            def _():
                low = pl.multiple_of((block + (lead + 1 - n)) * BLK, BLK)
                span = pl.ds(low, n * BLK)

                def head(h, carry):
                    g = h // (heads // KVH)
                    query_t = q_ref[h]
                    grad_t = g_ref[h]
                    scores = jnp.dot(k_ref[g, span, :], query_t, preferred_element_type=F32)
                    d_probs = jnp.dot(v_ref[g, span, :], grad_t, preferred_element_type=F32)
                    top = jnp.max(scores, axis=0, keepdims=True)
                    expon = jnp.exp(scores - top)
                    probs = expon * (1.0 / jnp.sum(expon, axis=0, keepdims=True))
                    delta = jnp.sum(probs * d_probs, axis=0, keepdims=True)
                    d_scores = (probs * (d_probs - delta)).astype(BF16)
                    dq_ref[h] = jnp.dot(kt_ref[g, :, span], d_scores, preferred_element_type=F32)
                    dk_acc[g, span, :] += jnp.dot(
                        d_scores, query_t.T, preferred_element_type=F32
                    )
                    dv_acc[g, span, :] += jnp.dot(
                        probs.astype(BF16), grad_t.T, preferred_element_type=F32
                    )
                    return carry

                lax.fori_loop(0, heads, head, 0)

        @pl.when(block == blocks - 1)
        def _():
            for g in range(KVH):
                dk_ref[g] = dk_acc[g].T
                dv_ref[g] = dv_acc[g].T

    return pl.pallas_call(
        body,
        name="attend_backward",
        out_shape=(
            jax.ShapeDtypeStruct((heads, size, rows), F32),
            jax.ShapeDtypeStruct((KVH, size, total), F32),
            jax.ShapeDtypeStruct((KVH, size, total), F32),
        ),
        grid_spec=pltpu.PrefetchScalarGridSpec(
            num_scalar_prefetch=1,
            grid=(blocks,),
            in_specs=[
                pl.BlockSpec((heads, size, BLK), lambda i, r: (0, 0, i)),
                pl.BlockSpec((heads, size, BLK), lambda i, r: (0, 0, i)),
                pl.BlockSpec((KVH, total, size), lambda i, r: (0, 0, 0)),
                pl.BlockSpec((KVH, size, total), lambda i, r: (0, 0, 0)),
                pl.BlockSpec((KVH, total, size), lambda i, r: (0, 0, 0)),
            ],
            out_specs=(
                pl.BlockSpec((heads, size, BLK), lambda i, r: (0, 0, i)),
                pl.BlockSpec((KVH, size, total), lambda i, r: (0, 0, 0)),
                pl.BlockSpec((KVH, size, total), lambda i, r: (0, 0, 0)),
            ),
            scratch_shapes=[
                pltpu.VMEM((KVH, total, size), F32),
                pltpu.VMEM((KVH, total, size), F32),
            ],
        ),
        cost_estimate=pl.CostEstimate(
            flops=64 * heads * rows * total * size,
            transcendentals=heads * rows * total,
            bytes_accessed=8 * heads * rows * size,
        ),
    )(runs, queries_t, grads_t, keys, keys_t, values)


def contract(left, right, left_dim, right_dim):
    return lax.dot_general(
        left, right, (((left_dim,), (right_dim,)), ((), ())), preferred_element_type=F32
    )


def rotate(values, cosine, sine):
    half = HD // 2
    upper, lower = values[:, :half], values[:, half:]
    return jnp.concatenate(
        [upper * cosine - lower * sine, lower * cosine + upper * sine], axis=1
    )


def rms_unit(values, axis):
    scale = lax.rsqrt(jnp.mean(values * values, axis=axis, keepdims=True) + EPS)
    return (values * scale, scale)


def norm_back(grad, unit, scale, axis):
    return scale * (grad - unit * jnp.mean(grad * unit, axis=axis, keepdims=True))


def on_device(
    tokens,
    cotangent,
    seq_ids,
    block_ids,
    positions,
    first_gain,
    query_weight,
    query_bias,
    key_weight,
    key_bias,
    value_weight,
    value_bias,
    out_weight,
    second_gain,
    gate_weight,
    up_weight,
    down_weight,
):
    net = Net()
    seqs = net.seqs
    order_a, order_b = net.orders
    rows, width = tokens.shape
    kv_width = KVH * HD
    query_width = H * HD
    runs = block_ids[::BLK]
    own_half = net.seq // (seqs // 2) == net.half
    even = net.seq % 2 == 0

    attn_shard = jnp.concatenate([query_weight, key_weight, value_weight, out_weight], axis=1)
    attn_columns = attn_shard.shape[1]
    vectors = jnp.concatenate([first_gain, query_bias, key_bias, value_bias, second_gain])
    sizes = [
        first_gain.shape[0],
        query_bias.shape[0],
        key_bias.shape[0],
        value_bias.shape[0],
        second_gain.shape[0],
    ]
    ends = [sum(sizes[: i + 1]) for i in range(len(sizes))]
    shard = attn_shard.shape[0]
    attn_width = cut_width(attn_columns, net.reps)
    attn_piece = lax.dynamic_slice_in_dim(
        attn_shard, cut_offset(net.rep, attn_columns, net.reps), attn_width, 1
    )
    extra = pl.cdiv(vectors.shape[0], attn_width * 8) * 8
    vector_rows = jnp.pad(vectors, (0, extra * attn_width - vectors.shape[0])).reshape(
        extra, attn_width
    )
    attn_seq = net.gather_seq(jnp.concatenate([attn_piece, vector_rows], axis=0)).reshape(
        seqs, shard + extra, attn_width
    )
    vector_all = attn_seq[:, shard:].reshape(seqs, -1).astype(F32)
    attn_seq = attn_seq[:, :shard].reshape(seqs * shard, attn_width)
    gain_one, query_bias_f, key_bias_f, value_bias_f, gain_two = [
        vector_all[:, e - s : e].reshape(-1) for s, e in zip(sizes, ends)
    ]
    top, low = attn_seq[: seqs * shard // 2], attn_seq[seqs * shard // 2 :]
    pieces = [net.spread(top, order_a), net.spread(low, order_b)]
    pieces = [
        [v for m in range(net.pairs) for v in (group[m], net.flip(group[m], 1))]
        for group in pieces
    ]
    part = seqs * shard // 2
    attn_full = jnp.concatenate(
        [
            assemble(
                net,
                [(0, attn_columns, net.reps, group)],
                attn_columns,
                lambda place: place[0],
                part // 2,
                2,
                lambda i, p: i,
            )
            for group in pieces
        ],
        axis=0,
    )
    proj_full = attn_full[:, : query_width + 2 * kv_width]
    out_full = attn_full[:, query_width + 2 * kv_width :]

    units = gate_weight.shape[1] // 2
    unit_width = cut_width(units, net.pairs)

    def gather_units(weight):
        start = net.half * units + cut_offset(net.pair, units, net.pairs)
        return lax.dynamic_slice_in_dim(weight, start, unit_width, 1)

    both_seq = net.gather_seq(
        jnp.concatenate([gather_units(gate_weight), gather_units(up_weight)], axis=0)
    ).reshape(seqs, 2, shard, unit_width)
    both_seq = jnp.concatenate([both_seq, both_seq], axis=0)
    both_seq = lax.dynamic_slice_in_dim(both_seq, net.seq + 1, seqs - 1, 0)
    gate_seq = both_seq[:, 0].reshape((seqs - 1) * shard, unit_width)
    up_seq = both_seq[:, 1].reshape((seqs - 1) * shard, unit_width)
    tiles = width // LANES
    split = pl.cdiv(tiles, 2) * LANES
    colours = [(0, split, order_a), (split, width - split, order_b)]
    down_piece = jnp.concatenate(
        [
            lax.dynamic_slice_in_dim(
                down_weight,
                start + cut_offset(net.pair, span, net.pairs),
                cut_width(span, net.pairs),
                1,
            )
            for start, span, _ in colours
        ],
        axis=1,
    )
    down_piece = after(down_piece, gate_seq, up_seq)
    held = jnp.where(own_half, down_piece, net.flip_seq(down_piece, seqs // 2))
    other = net.flip_seq(held, 1)
    down_seq = jnp.concatenate(
        [jnp.where(even, held, other), jnp.where(even, other, held)], axis=0
    )

    cotangent_both = jnp.concatenate([cotangent, net.flip(cotangent, 1)], axis=0)

    tokens_wide = tokens.astype(F32)
    unit_one, scale_one = rms_unit(tokens_wide, 1)
    normed_one = (unit_one * gain_one).astype(BF16)
    freqs = ROPE_BASE ** (-(jnp.arange(HD // 2, dtype=F32) * 2.0 / HD))
    angles = freqs[:, None] * positions.astype(F32)[None, :]
    cosine, sine = jnp.cos(angles), jnp.sin(angles)
    bias = jnp.concatenate([query_bias_f, key_bias_f, value_bias_f])
    proj_t = contract(proj_full, normed_one, 0, 1) + bias[:, None]
    factor = HD ** (-0.5)
    queries_t = rotate(proj_t[:query_width].reshape(H, HD, rows), cosine, sine)
    queries_t = (queries_t.astype(BF16).astype(F32) * factor).astype(BF16)
    keys_own = rotate(
        proj_t[query_width : query_width + kv_width].reshape(KVH, HD, rows), cosine, sine
    ).astype(BF16)
    values_own = proj_t[query_width + kv_width :].astype(BF16)
    kv_own = jnp.concatenate([keys_own.reshape(kv_width, rows), values_own], axis=0)
    gate_parts, up_parts = {0: gate_seq}, {0: up_seq}
    bits_a, bits_b = list(order_a), list(order_b)
    net.grow(gate_parts, bits_a[0])
    net.grow(up_parts, bits_b[0])
    halo = []
    need = (SEQ_BLOCKS - 1) * BLK
    step = 1
    while need > 0:
        take = min(need, rows)
        halo.insert(0, net.slide(kv_own[:, rows - take :], step))
        need -= take
        step += 1
    kv_t = jnp.concatenate(halo + [kv_own], axis=1).reshape(2 * KVH, HD, -1)
    kv_t = after(kv_t, gate_parts, up_parts)
    for bit_a, bit_b in zip(bits_a[1:], bits_b[1:]):
        net.grow(gate_parts, bit_a)
        net.grow(up_parts, bit_b)
    gate_pieces = [gate_parts[m] for m in range(net.pairs)]
    up_pieces = [up_parts[m] for m in range(net.pairs)]
    kv = jnp.transpose(kv_t, (0, 2, 1))
    attended_t = attend_forward(queries_t, kv[:KVH], kv_t[KVH:], runs)
    attended_t = attended_t.reshape(query_width, rows)
    mixed = tokens_wide + contract(attended_t, out_full, 0, 0)

    unit_two, scale_two = rms_unit(mixed, 1)
    normed_two = (unit_two * gain_two).astype(BF16)
    normed_both = jnp.concatenate([normed_two, net.flip(normed_two, 1)], axis=0)
    pair_index = lambda place: place[0] // 2
    down_seq = after(down_seq, gate_pieces, up_pieces)
    down_pieces, at = [], 0
    for start, span, order in colours:
        piece_width = cut_width(span, net.pairs)
        piece = down_seq[:, at : at + piece_width]
        down_pieces.append((start, span, net.pairs, net.spread(piece, order)))
        at += piece_width
    next_shard = lambda i, p: (p[1] + i) % seqs

    def assemble_units(pieces, weight):
        own = lax.dynamic_slice_in_dim(weight, net.half * units, units, 1)
        region = (0, units, net.pairs, pieces)
        return assemble(net, [region], units, pair_index, shard, seqs, next_shard, own)

    gate_half = assemble_units(gate_pieces, gate_weight)
    up_half = assemble_units(up_pieces, up_weight)
    gate_pre = contract(normed_both, gate_half, 1, 0)
    up_pre = contract(normed_both, up_half, 1, 0)
    sigmoid_gate = jax.nn.sigmoid(gate_pre)
    silu_gate = gate_pre * sigmoid_gate
    hidden = (silu_gate * up_pre).astype(BF16)
    grad_down = weight_grad(net, cotangent_both.T, hidden, colours, True)
    fold_down = [Fold(net, g, order) for g, (_, _, order) in zip(grad_down, colours)]
    down_half = assemble(
        net, down_pieces, width, pair_index, units // 4, 4, lambda i, p: i
    )
    output_both = contract(hidden, down_half, 1, 0)
    output = (mixed + output_both[:rows] + net.flip(output_both[rows:], 1)).astype(BF16)
    d_hidden = contract(after(cotangent_both, grad_down), down_half, 1, 1)
    d_gate = (d_hidden * up_pre * sigmoid_gate * (1.0 + gate_pre * (1.0 - sigmoid_gate))).astype(
        BF16
    )
    d_up = (d_hidden * silu_gate).astype(BF16)
    normed_both_t = normed_both.T
    for fold in fold_down:
        fold.step()
    grad_gate = weight_grad(net, normed_both_t, d_gate, [(0, units, order_a)], False)
    grad_up = weight_grad(net, normed_both_t, d_up, [(0, units, order_b)], False)
    fold_units = [Fold(net, grad_gate[0], order_a), Fold(net, grad_up[0], order_b)]
    d_gate, d_up = after((d_gate, d_up), grad_gate, grad_up, *[f.state() for f in fold_down])
    d_normed_both = contract(d_gate, gate_half, 1, 1) + contract(d_up, up_half, 1, 1)
    d_normed_two = d_normed_both[:rows] + net.flip(d_normed_both[rows:], 1)
    grad_gain_two = jnp.sum(d_normed_two * unit_two, axis=0)
    d_mixed = cotangent.astype(F32) + norm_back(d_normed_two * gain_two, unit_two, scale_two, 1)

    for fold in fold_down:
        fold.rest()
    d_mixed = after(d_mixed, *[f.keep for f in fold_down])
    for fold in fold_units:
        fold.step()
    piece = jnp.concatenate([f.keep[0] for f in fold_down], axis=0).T
    span = piece.shape[0] // 2
    first, second = piece[:span], piece[span:]
    mine = jnp.where(even, first, second)
    mine = mine.astype(F32) + net.flip_seq(jnp.where(even, second, first), 1).astype(F32)
    mine = (mine + net.flip_seq(mine.astype(BF16), seqs // 2).astype(F32)).astype(BF16)
    mine = jnp.where(own_half, mine, net.flip(mine, 1))

    d_branch = d_mixed.astype(BF16)
    d_attended_t = contract(out_full, d_branch, 1, 1).astype(BF16)
    d_query_t, d_key_t, d_value_t = attend_backward(
        queries_t, d_attended_t.reshape(H, HD, rows), kv[:KVH], kv_t[:KVH], kv[KVH:], runs
    )
    d_key_t, d_value_t = after((d_key_t, d_value_t), *[f.state() for f in fold_units])
    d_kv = jnp.concatenate(
        [d_key_t.reshape(kv_width, -1), d_value_t.reshape(kv_width, -1)], axis=0
    )
    lead = (SEQ_BLOCKS - 1) * BLK
    d_kv_own = d_kv[:, lead:]
    need = lead
    step = 1
    while need > 0:
        take = min(need, rows)
        back = net.slide(d_kv[:, need - take : need].astype(BF16), -step).astype(F32)
        d_kv_own = d_kv_own + jnp.pad(back, ((0, 0), (rows - take, 0)))
        need -= take
        step += 1
    d_query_pre_t = rotate(d_query_t * factor, cosine, -sine).reshape(query_width, rows)
    d_key_pre_t = rotate(d_kv_own[:kv_width].reshape(KVH, HD, rows), cosine, -sine)
    d_proj_t = jnp.concatenate(
        [d_query_pre_t, d_key_pre_t.reshape(kv_width, rows), d_kv_own[kv_width:]], axis=0
    ).astype(BF16)
    d_proj = d_proj_t.T
    grad_bias = jnp.sum(d_proj_t.astype(F32), axis=1)
    d_normed_one = contract(d_proj, proj_full, 1, 1)
    grad_gain_one = jnp.sum(d_normed_one * unit_one, axis=0)
    tokens_grad = (d_mixed + norm_back(d_normed_one * gain_one, unit_one, scale_one, 1)).astype(
        BF16
    )

    both = jnp.concatenate(
        [f.rest().reshape(seqs, shard, unit_width) for f in fold_units], axis=1
    ).reshape(-1, unit_width)
    both = lax.psum_scatter(both, "seq", scatter_dimension=0, tiled=True)
    both = lax.all_gather(both, "rep", axis=0)
    moves = [
        (2 * k + h, 0, unit_width, h * units + min(k * unit_width, units - unit_width))
        for k in range(net.pairs)
        for h in range(2)
    ]
    sum_gate = widen(both, 2 * units, moves, 0, shard)
    sum_up = widen(both, 2 * units, moves, shard, shard)
    mine = lax.all_gather(mine, "rep", axis=0, axis_index_groups=net.same_half)
    moves, at = [], 0
    for start, span, _ in colours:
        w = cut_width(span, net.pairs)
        moves += [(k, at, w, start + min(k * w, span - w)) for k in range(net.pairs)]
        at += w
    sum_down = widen(mine, width, moves, 0, mine.shape[1])

    grad_qkv = contract(normed_one, d_proj, 0, 0)
    grad_out = contract(attended_t, d_branch, 1, 0)
    grad_attn = jnp.concatenate([grad_qkv, grad_out], axis=1).astype(BF16)
    grad_attn = grad_attn.reshape(seqs, shard, attn_columns)
    pieces_of = lambda v: v.reshape(seqs, -1)
    small = jnp.concatenate(
        [
            pieces_of(grad_gain_one),
            pieces_of(grad_bias[:query_width]),
            pieces_of(grad_bias[query_width : query_width + kv_width]),
            pieces_of(grad_bias[query_width + kv_width :]),
            pieces_of(grad_gain_two),
        ],
        axis=1,
    ).astype(BF16)
    pad = 32
    small = jnp.pad(small, ((0, 0), (0, attn_columns - small.shape[1])))[:, None]
    small = jnp.pad(small, ((0, 0), (0, pad - 1), (0, 0)))
    grad_attn = jnp.concatenate([grad_attn, small], axis=1).reshape(-1, attn_columns)
    if attn_columns % (net.reps * LANES) == 0:
        stack = jnp.transpose(
            grad_attn.reshape(-1, net.reps, attn_width), (1, 0, 2)
        )
    else:
        stack = jnp.stack(
            [
                grad_attn[:, o : o + attn_width]
                for o in (
                    min(k * attn_width, attn_columns - attn_width) for k in range(net.reps)
                )
            ]
        )
    stack = lax.psum_scatter(stack, "rep", scatter_dimension=0, tiled=True)[0]
    stack = lax.psum_scatter(stack, "seq", scatter_dimension=0, tiled=True)
    stack = lax.all_gather(stack, "rep", axis=0)
    moves = [
        (k, 0, attn_width, min(k * attn_width, attn_columns - attn_width))
        for k in range(net.reps)
    ]
    sum_attn = widen(stack, attn_columns, moves, 0, stack.shape[1])
    row = sum_attn[shard]
    sum_gain_one, sum_query_bias, sum_key_bias, sum_value_bias, sum_gain_two = [
        row[e - s : e] for s, e in zip(sizes, ends)
    ]
    a, b, c = query_width, query_width + kv_width, query_width + 2 * kv_width
    return (
        output,
        tokens_grad,
        sum_gain_one,
        sum_attn[:shard, :a],
        sum_query_bias,
        sum_attn[:shard, a:b],
        sum_key_bias,
        sum_attn[:shard, b:c],
        sum_value_bias,
        sum_attn[:shard, c:],
        sum_gain_two,
        sum_gate,
        sum_up,
        sum_down,
    )


def solution(mesh):
    both = ("rep", "seq")
    return jax.shard_map(
        on_device,
        mesh=mesh,
        in_specs=(
            P(both, None),
            P(both, None),
            P(both),
            P(both),
            P(both),
            P("seq"),
            P("seq", None),
            P("seq"),
            P("seq", None),
            P("seq"),
            P("seq", None),
            P("seq"),
            P("seq", None),
            P("seq"),
            P("seq", None),
            P("seq", None),
            P("seq", None),
        ),
        out_specs=(
            P(both, None),
            P(both, None),
            P("seq"),
            P("seq", None),
            P("seq"),
            P("seq", None),
            P("seq"),
            P("seq", None),
            P("seq"),
            P("seq", None),
            P("seq"),
            P("seq", None),
            P("seq", None),
            P("seq", None),
        ),
        check_vma=False,
    )
```

```python
import jax
import jax.numpy as jnp
from jax import lax
from jax.experimental import pallas as pl
from jax.experimental.pallas import tpu as pltpu
from jax.sharding import PartitionSpec as P

H = 14
KVH = 2
HD = 64
BLK = 256
SEQ_BLOCKS = 4
LANES = 128

EPS = 1e-06
ROPE_BASE = 1000000.0

F32 = jnp.float32
BF16 = jnp.bfloat16


class Net:
    def __init__(self):
        self.reps = lax.axis_size("rep")
        self.seqs = lax.axis_size("seq")
        self.rep = lax.axis_index("rep").astype(jnp.int32)
        self.seq = lax.axis_index("seq").astype(jnp.int32)
        self.place = jnp.stack([self.rep, self.seq])
        self.pairs = self.reps // 2
        self.half = self.rep % 2
        self.pair = self.rep // 2
        bits = []
        bit = 1
        while bit < self.pairs:
            bits.append(bit)
            bit *= 2
        self.orders = (tuple(bits), tuple(bits[::-1]))
        self.same_half = [[2 * k + c for k in range(self.pairs)] for c in range(2)]

    def flip(self, value, bit):
        return lax.ppermute(value, "rep", [(i, i ^ bit) for i in range(self.reps)])

    def flip_seq(self, value, bit):
        return lax.ppermute(value, "seq", [(i, i ^ bit) for i in range(self.seqs)])

    def slide(self, value, step):
        pairs = [(i, i + step) for i in range(self.seqs) if 0 <= i + step < self.seqs]
        return lax.ppermute(value, "seq", pairs)

    def gather_seq(self, value):
        return lax.all_gather(value, "seq", axis=0, tiled=True)

    def spread(self, piece, order):
        held = {0: piece}
        for bit in order:
            held.update({m ^ bit: self.flip(v, 2 * bit) for m, v in list(held.items())})
        return [held[m] for m in range(self.pairs)]

    def grow(self, held, bit):
        held.update({m ^ bit: self.flip(v, 2 * bit) for m, v in list(held.items())})


class Fold:
    def __init__(self, net, parts, order, scale=2):
        self.net = net
        self.scale = scale
        self.keep, self.send = parts
        self.bits = list(order)

    def launch(self):
        self.got = self.net.flip(self.send, self.scale * self.bits.pop(0))

    def collect(self):
        half = self.keep.shape[0] // 2
        total = lambda own, got: (own.astype(F32) + got.astype(F32)).astype(BF16)
        if half == 0:
            self.keep = total(self.keep, self.got)
            return
        self.send = total(self.keep[half:], self.got[half:])
        self.keep = total(self.keep[:half], self.got[:half])

    def until_last(self):
        while self.bits:
            self.collect()
            self.launch()


def got_of(folds):
    return [f.got for f in folds]


def launch_all(folds):
    for fold in folds:
        fold.launch()


def collect_all(folds):
    for fold in folds:
        fold.collect()


def after(value, *others):
    return lax.optimization_barrier((value, others))[0]


def cut_width(columns, parts):
    return pl.cdiv(columns // LANES, parts) * LANES


def cut_offset(index, columns, parts):
    width = cut_width(columns, parts)
    return jnp.minimum(index * width, columns - width)


def piece_of_rank(rank, order):
    count = len(order)
    piece = 0
    for at, bit in enumerate(order):
        piece = piece | (((rank >> (count - 1 - at)) & 1) * bit)
    return piece


def assemble(net, regions, columns, index, rows, steps, place_of, own=None, dtype=BF16):
    flat = [p for region in regions for p in region[3]]
    skip = 0 if own is None else 1

    def body(place, *refs):
        out = refs[-1]

        def fill():
            at = 0
            for start, span, parts, pieces in regions:
                for m, piece in enumerate(pieces):
                    base = start(place) if callable(start) else start
                    offset = base + cut_offset(index(place) ^ m, span, parts)
                    col = pl.multiple_of(offset, LANES)
                    out[:, pl.ds(col, piece.shape[1])] = refs[at][...].astype(dtype)
                    at += 1

        if own is None:
            fill()
        else:

            @pl.when(pl.program_id(0) == 0)
            def _():
                out[...] = refs[-2][...]

            @pl.when(pl.program_id(0) > 0)
            def _():
                fill()

    in_specs = [
        pl.BlockSpec((rows, p.shape[1]), lambda i, p: (jnp.maximum(i - skip, 0), 0)) for p in flat
    ]
    if own is not None:
        in_specs.append(pl.BlockSpec((rows, columns), lambda i, p: (0, 0)))
        flat = flat + [own]
    return pl.pallas_call(
        body,
        name="assemble",
        out_shape=jax.ShapeDtypeStruct((rows * steps, columns), dtype),
        grid_spec=pltpu.PrefetchScalarGridSpec(
            num_scalar_prefetch=1,
            grid=(steps,),
            in_specs=in_specs,
            out_specs=pl.BlockSpec((rows, columns), lambda i, p: (place_of(i, p), 0)),
        ),
        cost_estimate=pl.CostEstimate(
            flops=0, transcendentals=0, bytes_accessed=4 * rows * steps * columns
        ),
    )(net.place, *flat)


def pieces_call(net, body, name, left, right, shapes):
    half = net.pairs // 2
    out_shape, out_specs = [], []
    for shape in shapes:
        out_shape += [jax.ShapeDtypeStruct((half,) + shape, BF16)] * 2
        out_specs += [
            pl.BlockSpec((1,) + shape, lambda i, p: (jnp.minimum(i, half - 1), 0, 0)),
            pl.BlockSpec((1,) + shape, lambda i, p: (jnp.maximum(i - half, 0), 0, 0)),
        ]

    def whole(place, left_ref, right_ref, *outs):
        step = pl.program_id(0)
        values = body(step, place[0] // 2, left_ref, right_ref)

        @pl.when(step < half)
        def _():
            for k, value in enumerate(values):
                outs[2 * k][0] = value

        @pl.when(step >= half)
        def _():
            for k, value in enumerate(values):
                outs[2 * k + 1][0] = value

    outs = pl.pallas_call(
        whole,
        name=name,
        out_shape=out_shape,
        grid_spec=pltpu.PrefetchScalarGridSpec(
            num_scalar_prefetch=1,
            grid=(net.pairs,),
            in_specs=[
                pl.BlockSpec(left.shape, lambda i, p: (0, 0)),
                pl.BlockSpec(right.shape, lambda i, p: (0, 0)),
            ],
            out_specs=out_specs,
        ),
        cost_estimate=pl.CostEstimate(
            flops=2 * left.shape[0] * left.shape[1] * right.shape[1],
            transcendentals=0,
            bytes_accessed=2 * (left.size + right.size + left.shape[0] * right.shape[1]),
        ),
    )(net.place, left, right)
    return [tuple(outs[2 * k : 2 * k + 2]) for k in range(len(shapes))]


def unit_grad(net, left_t, right):
    total, tokens = left_t.shape
    columns = right.shape[1]
    width = cut_width(columns, net.pairs)
    start = lambda i: cut_offset(i, columns, net.pairs)

    def body(left_ref, right_ref, out_ref):
        at = pl.multiple_of(start(pl.program_id(0)), LANES)
        out_ref[0] = jnp.dot(
            left_ref[...], right_ref[:, pl.ds(at, width)], preferred_element_type=F32
        ).astype(BF16)

    return pl.pallas_call(
        body,
        name="unit_grad",
        out_shape=jax.ShapeDtypeStruct((net.pairs, total, width), BF16),
        grid=(net.pairs,),
        in_specs=[
            pl.BlockSpec((total, tokens), lambda i: (0, 0)),
            pl.BlockSpec((tokens, columns), lambda i: (0, 0)),
        ],
        out_specs=pl.BlockSpec((1, total, width), lambda i: (i, 0, 0)),
        cost_estimate=pl.CostEstimate(
            flops=2 * total * tokens * columns,
            transcendentals=0,
            bytes_accessed=2 * (left_t.size + right.size + total * columns),
        ),
    )(left_t, right)


def down_grad(net, left_t, right, colours):
    widths = [cut_width(span, net.pairs) for _, span, _ in colours]
    columns = right.shape[1]

    def body(step, pair, left_ref, right_ref):
        slabs = []
        for (start, span, order), width in zip(colours, widths):
            piece = pair ^ piece_of_rank(step, order)
            at = pl.multiple_of(start + cut_offset(piece, span, net.pairs), LANES)
            slabs.append(left_ref[pl.ds(at, width), :])
        val = jnp.dot(
            jnp.concatenate(slabs, axis=0), right_ref[...], preferred_element_type=F32
        ).T.astype(BF16)
        values, at = [], 0
        for width in widths:
            values.append(val[:, at : at + width])
            at += width
        return values

    return pieces_call(net, body, "down_grad", left_t, right, [(columns, w) for w in widths])


def attn_grad(net, first_t, first_right, second_t, second_right, extra, orders):
    reps, seqs = net.reps, net.seqs
    rows = first_t.shape[0] // seqs
    pad = extra.shape[1]
    part = (rows + pad) // len(orders)
    split = first_right.shape[1]
    columns = split + second_right.shape[1]
    width = cut_width(columns, reps)
    half = reps // 2

    def body(place, a_ref, b_ref, c_ref, d_ref, e_ref, *refs):
        outs, full = refs[:-1], refs[-1]
        step = pl.program_id(0)

        @pl.when(step == 0)
        def _():
            first = jnp.dot(a_ref[...], b_ref[...], preferred_element_type=F32).astype(BF16)
            second = jnp.dot(c_ref[...], d_ref[...], preferred_element_type=F32).astype(BF16)
            for s in range(seqs):
                full[s, :rows, :split] = first[s * rows : (s + 1) * rows]
                full[s, :rows, split:] = second[s * rows : (s + 1) * rows]
                full[s, rows:, :] = e_ref[s]

        for k, order in enumerate(orders):
            piece = place[0] ^ piece_of_rank(step, order)
            at = pl.multiple_of(cut_offset(piece, columns, reps), LANES)

            @pl.when(step < half)
            def _():
                outs[2 * k][0] = full[:, k * part : (k + 1) * part, pl.ds(at, width)]

            @pl.when(step >= half)
            def _():
                outs[2 * k + 1][0] = full[:, k * part : (k + 1) * part, pl.ds(at, width)]

    shape = (seqs, part, width)
    out_shape, out_specs = [], []
    for _ in orders:
        out_shape += [jax.ShapeDtypeStruct((half,) + shape, BF16)] * 2
        out_specs += [
            pl.BlockSpec((1,) + shape, lambda i, p: (jnp.minimum(i, half - 1), 0, 0, 0)),
            pl.BlockSpec((1,) + shape, lambda i, p: (jnp.maximum(i - half, 0), 0, 0, 0)),
        ]
    args = (first_t, first_right, second_t, second_right)
    outs = pl.pallas_call(
        body,
        name="attn_grad",
        out_shape=out_shape,
        grid_spec=pltpu.PrefetchScalarGridSpec(
            num_scalar_prefetch=1,
            grid=(reps,),
            in_specs=[pl.BlockSpec(v.shape, lambda i, p: (0, 0)) for v in args]
            + [pl.BlockSpec(extra.shape, lambda i, p: (0, 0, 0))],
            out_specs=out_specs,
            scratch_shapes=[pltpu.VMEM((seqs, rows + pad, columns), BF16)],
        ),
        cost_estimate=pl.CostEstimate(
            flops=2 * first_t.size * columns,
            transcendentals=0,
            bytes_accessed=2 * (seqs * (rows + pad) * columns + 4 * first_t.size),
        ),
    )(net.place, *args, extra)
    return [tuple(outs[2 * k : 2 * k + 2]) for k in range(len(orders))]


def attend_forward(queries_t, keys, values_t, runs):
    heads, size, rows = queries_t.shape
    total = keys.shape[1]
    blocks = rows // BLK
    lead = total // BLK - blocks

    def body(runs_ref, q_ref, k_ref, v_ref, o_ref):
        block = pl.program_id(0)
        run = runs_ref[block]
        for n in range(1, SEQ_BLOCKS + 1):

            @pl.when(run == n - 1)
            def _():
                low = pl.multiple_of((block + (lead + 1 - n)) * BLK, BLK)

                def head(h, carry):
                    g = h // (heads // KVH)
                    scores = jnp.dot(
                        k_ref[g, pl.ds(low, n * BLK), :], q_ref[h], preferred_element_type=F32
                    )
                    top = jnp.max(scores, axis=0, keepdims=True)
                    expon = jnp.exp(scores - top)
                    norm = jnp.sum(expon, axis=0, keepdims=True)
                    out = jnp.dot(
                        v_ref[g, :, pl.ds(low, n * BLK)],
                        expon.astype(BF16),
                        preferred_element_type=F32,
                    )
                    o_ref[h] = (out / norm).astype(BF16)
                    return carry

                lax.fori_loop(0, heads, head, 0, unroll=2)

    return pl.pallas_call(
        body,
        name="attend_forward",
        out_shape=jax.ShapeDtypeStruct((heads, size, rows), BF16),
        grid_spec=pltpu.PrefetchScalarGridSpec(
            num_scalar_prefetch=1,
            grid=(blocks,),
            in_specs=[
                pl.BlockSpec((heads, size, BLK), lambda i, r: (0, 0, i)),
                pl.BlockSpec((KVH, total, size), lambda i, r: (0, 0, 0)),
                pl.BlockSpec((KVH, size, total), lambda i, r: (0, 0, 0)),
            ],
            out_specs=pl.BlockSpec((heads, size, BLK), lambda i, r: (0, 0, i)),
        ),
        cost_estimate=pl.CostEstimate(
            flops=32 * heads * rows * total * size,
            transcendentals=heads * rows * total,
            bytes_accessed=8 * heads * rows * size,
        ),
    )(runs, queries_t, keys, values_t)


def attend_backward(queries_t, grads_t, keys, keys_t, values, runs):
    heads, size, rows = queries_t.shape
    total = keys.shape[1]
    blocks = rows // BLK
    lead = total // BLK - blocks

    def body(runs_ref, q_ref, g_ref, k_ref, kt_ref, v_ref, dq_ref, dk_ref, dv_ref, dk_acc, dv_acc):
        block = pl.program_id(0)
        run = runs_ref[block]

        @pl.when(block == 0)
        def _():
            dk_acc[...] = jnp.zeros_like(dk_acc)
            dv_acc[...] = jnp.zeros_like(dv_acc)

        for n in range(1, SEQ_BLOCKS + 1):

            @pl.when(run == n - 1)
            def _():
                low = pl.multiple_of((block + (lead + 1 - n)) * BLK, BLK)
                span = pl.ds(low, n * BLK)

                def head(h, carry):
                    g = h // (heads // KVH)
                    query_t = q_ref[h]
                    grad_t = g_ref[h]
                    scores = jnp.dot(k_ref[g, span, :], query_t, preferred_element_type=F32)
                    d_probs = jnp.dot(v_ref[g, span, :], grad_t, preferred_element_type=F32)
                    top = jnp.max(scores, axis=0, keepdims=True)
                    expon = jnp.exp(scores - top)
                    probs = expon * (1.0 / jnp.sum(expon, axis=0, keepdims=True))
                    delta = jnp.sum(probs * d_probs, axis=0, keepdims=True)
                    d_scores = (probs * (d_probs - delta)).astype(BF16)
                    dq_ref[h] = jnp.dot(kt_ref[g, :, span], d_scores, preferred_element_type=F32)
                    dk_acc[g, span, :] += jnp.dot(
                        d_scores, query_t.T, preferred_element_type=F32
                    )
                    dv_acc[g, span, :] += jnp.dot(
                        probs.astype(BF16), grad_t.T, preferred_element_type=F32
                    )
                    return carry

                lax.fori_loop(0, heads, head, 0)

        @pl.when(block == blocks - 1)
        def _():
            for g in range(KVH):
                dk_ref[g] = dk_acc[g].T
                dv_ref[g] = dv_acc[g].T

    return pl.pallas_call(
        body,
        name="attend_backward",
        out_shape=(
            jax.ShapeDtypeStruct((heads, size, rows), F32),
            jax.ShapeDtypeStruct((KVH, size, total), F32),
            jax.ShapeDtypeStruct((KVH, size, total), F32),
        ),
        grid_spec=pltpu.PrefetchScalarGridSpec(
            num_scalar_prefetch=1,
            grid=(blocks,),
            in_specs=[
                pl.BlockSpec((heads, size, BLK), lambda i, r: (0, 0, i)),
                pl.BlockSpec((heads, size, BLK), lambda i, r: (0, 0, i)),
                pl.BlockSpec((KVH, total, size), lambda i, r: (0, 0, 0)),
                pl.BlockSpec((KVH, size, total), lambda i, r: (0, 0, 0)),
                pl.BlockSpec((KVH, total, size), lambda i, r: (0, 0, 0)),
            ],
            out_specs=(
                pl.BlockSpec((heads, size, BLK), lambda i, r: (0, 0, i)),
                pl.BlockSpec((KVH, size, total), lambda i, r: (0, 0, 0)),
                pl.BlockSpec((KVH, size, total), lambda i, r: (0, 0, 0)),
            ),
            scratch_shapes=[
                pltpu.VMEM((KVH, total, size), F32),
                pltpu.VMEM((KVH, total, size), F32),
            ],
        ),
        cost_estimate=pl.CostEstimate(
            flops=64 * heads * rows * total * size,
            transcendentals=heads * rows * total,
            bytes_accessed=8 * heads * rows * size,
        ),
    )(runs, queries_t, grads_t, keys, keys_t, values)


def contract(left, right, left_dim, right_dim):
    return lax.dot_general(
        left, right, (((left_dim,), (right_dim,)), ((), ())), preferred_element_type=F32
    )


def rotate(values, cosine, sine):
    half = HD // 2
    upper, lower = values[:, :half], values[:, half:]
    return jnp.concatenate(
        [upper * cosine - lower * sine, lower * cosine + upper * sine], axis=1
    )


def rms_unit(values, axis):
    scale = lax.rsqrt(jnp.mean(values * values, axis=axis, keepdims=True) + EPS)
    return (values * scale, scale)


def norm_back(grad, unit, scale, axis):
    return scale * (grad - unit * jnp.mean(grad * unit, axis=axis, keepdims=True))


def on_device(
    tokens,
    cotangent,
    seq_ids,
    block_ids,
    positions,
    first_gain,
    query_weight,
    query_bias,
    key_weight,
    key_bias,
    value_weight,
    value_bias,
    out_weight,
    second_gain,
    gate_weight,
    up_weight,
    down_weight,
):
    net = Net()
    seqs = net.seqs
    order_a, order_b = net.orders
    rows, width = tokens.shape
    kv_width = KVH * HD
    query_width = H * HD
    runs = block_ids[::BLK]
    own_half = net.seq // (seqs // 2) == net.half
    even = net.seq % 2 == 0

    attn_shard = jnp.concatenate([query_weight, key_weight, value_weight, out_weight], axis=1)
    attn_columns = attn_shard.shape[1]
    vectors = jnp.concatenate([first_gain, query_bias, key_bias, value_bias, second_gain])
    sizes = [
        first_gain.shape[0],
        query_bias.shape[0],
        key_bias.shape[0],
        value_bias.shape[0],
        second_gain.shape[0],
    ]
    ends = [sum(sizes[: i + 1]) for i in range(len(sizes))]
    shard = attn_shard.shape[0]
    attn_width = cut_width(attn_columns, net.reps)
    units = gate_weight.shape[1] // 2
    unit_width = cut_width(units, net.pairs)

    def cut_units(weight):
        start = net.half * units + cut_offset(net.pair, units, net.pairs)
        return lax.dynamic_slice_in_dim(weight, start, unit_width, 1)

    unit_pieces = jnp.concatenate([cut_units(gate_weight), cut_units(up_weight)], axis=0)
    attn_piece = lax.dynamic_slice_in_dim(
        attn_shard, cut_offset(net.rep, attn_columns, net.reps), attn_width, 1
    )
    attn_piece = after(attn_piece, unit_pieces)
    extra = pl.cdiv(vectors.shape[0], attn_width * 8) * 8
    vector_rows = jnp.pad(vectors, (0, extra * attn_width - vectors.shape[0])).reshape(
        extra, attn_width
    )
    attn_seq = net.gather_seq(jnp.concatenate([attn_piece, vector_rows], axis=0)).reshape(
        seqs, shard + extra, attn_width
    )
    vector_all = attn_seq[:, shard:].reshape(seqs, -1).astype(F32)
    attn_seq = attn_seq[:, :shard].reshape(seqs * shard, attn_width)
    gain_one, query_bias_f, key_bias_f, value_bias_f, gain_two = [
        vector_all[:, e - s : e].reshape(-1) for s, e in zip(sizes, ends)
    ]
    top, low = attn_seq[: seqs * shard // 2], attn_seq[seqs * shard // 2 :]
    pieces = [net.spread(top, order_a), net.spread(low, order_b)]
    pieces = [
        [v for m in range(net.pairs) for v in (group[m], net.flip(group[m], 1))]
        for group in pieces
    ]
    part = seqs * shard // 2
    attn_full = jnp.concatenate(
        [
            assemble(
                net,
                [(0, attn_columns, net.reps, group)],
                attn_columns,
                lambda place: place[0],
                part // 2,
                2,
                lambda i, p: i,
            )
            for group in pieces
        ],
        axis=0,
    )
    proj_full = attn_full[:, : query_width + 2 * kv_width]
    out_full = attn_full[:, query_width + 2 * kv_width :]

    both_seq = net.gather_seq(unit_pieces).reshape(seqs, 2, shard, unit_width)
    both_seq = jnp.concatenate([both_seq, both_seq], axis=0)
    both_seq = lax.dynamic_slice_in_dim(both_seq, net.seq + 1, seqs - 1, 0)
    gate_seq = both_seq[:, 0].reshape((seqs - 1) * shard, unit_width)
    up_seq = both_seq[:, 1].reshape((seqs - 1) * shard, unit_width)

    shard_units = down_weight.shape[0]
    tiles = width // LANES
    split = pl.cdiv(tiles, 2) * LANES
    colours = [(0, split, order_a), (split, width - split, order_b)]
    down_cuts = [
        lax.dynamic_slice_in_dim(
            down_weight,
            start + cut_offset(net.pair, span, net.pairs),
            cut_width(span, net.pairs),
            1,
        )
        for start, span, _ in colours
    ]

    cotangent_both = jnp.concatenate([cotangent, net.flip(cotangent, 1)], axis=0)

    tokens_wide = tokens.astype(F32)
    unit_one, scale_one = rms_unit(tokens_wide, 1)
    normed_one = (unit_one * gain_one).astype(BF16)
    freqs = ROPE_BASE ** (-(jnp.arange(HD // 2, dtype=F32) * 2.0 / HD))
    angles = freqs[:, None] * positions.astype(F32)[None, :]
    cosine, sine = jnp.cos(angles), jnp.sin(angles)
    bias = jnp.concatenate([query_bias_f, key_bias_f, value_bias_f])
    proj_t = contract(proj_full, normed_one, 0, 1) + bias[:, None]
    factor = HD ** (-0.5)
    queries_t = rotate(proj_t[:query_width].reshape(H, HD, rows), cosine, sine)
    queries_t = (queries_t.astype(BF16).astype(F32) * factor).astype(BF16)
    keys_own = rotate(
        proj_t[query_width : query_width + kv_width].reshape(KVH, HD, rows), cosine, sine
    ).astype(BF16)
    values_own = proj_t[query_width + kv_width :].astype(BF16)
    kv_own = jnp.concatenate([keys_own.reshape(kv_width, rows), values_own], axis=0)
    gate_parts, up_parts = {0: gate_seq}, {0: up_seq}
    bits_a, bits_b = list(order_a), list(order_b)
    net.grow(gate_parts, bits_a[0])
    net.grow(up_parts, bits_b[0])
    halo = []
    need = (SEQ_BLOCKS - 1) * BLK
    step = 1
    while need > 0:
        take = min(need, rows)
        halo.insert(0, net.slide(kv_own[:, rows - take :], step))
        need -= take
        step += 1
    kv_t = jnp.concatenate(halo + [kv_own], axis=1).reshape(2 * KVH, HD, -1)
    kv_t = after(kv_t, gate_parts, up_parts)
    down_cuts = after(down_cuts, kv_t)
    down_got = [net.flip_seq(v, seqs // 2) for v in down_cuts]
    for bit_a, bit_b in zip(bits_a[1:], bits_b[1:]):
        net.grow(gate_parts, bit_a)
        net.grow(up_parts, bit_b)
    gate_pieces = [gate_parts[m] for m in range(net.pairs)]
    up_pieces = [up_parts[m] for m in range(net.pairs)]
    kv = jnp.transpose(kv_t, (0, 2, 1))
    attended_t = attend_forward(queries_t, kv[:KVH], kv_t[KVH:], runs)
    attended_t = after(attended_t.reshape(query_width, rows), down_got)
    held = [jnp.where(own_half, u, v) for u, v in zip(down_cuts, down_got)]
    other = [net.flip_seq(v, 1) for v in held]
    mixed = tokens_wide + contract(attended_t, out_full, 0, 0)

    unit_two, scale_two = rms_unit(mixed, 1)
    normed_two = (unit_two * gain_two).astype(BF16)
    normed_both = jnp.concatenate([normed_two, net.flip(normed_two, 1)], axis=0)
    pair_index = lambda place: place[0] // 2
    next_shard = lambda i, p: (p[1] + i) % seqs

    def assemble_units(pieces, weight):
        own = lax.dynamic_slice_in_dim(weight, net.half * units, units, 1)
        region = (0, units, net.pairs, pieces)
        return assemble(net, [region], units, pair_index, shard, seqs, next_shard, own)

    gate_half = assemble_units(gate_pieces, gate_weight)
    up_half = assemble_units(up_pieces, up_weight)
    gate_pre = contract(normed_both, gate_half, 1, 0)
    down_seq = [
        jnp.concatenate([jnp.where(even, u, v), jnp.where(even, v, u)], axis=0)
        for u, v in zip(held, other)
    ]
    down_parts = [{0: v} for v in down_seq]
    for held, order in zip(down_parts, (order_a, order_b)):
        net.grow(held, order[0])
    up_pre = contract(after(normed_both, other, gate_pre), up_half, 1, 0)
    sigmoid_gate = jax.nn.sigmoid(gate_pre)
    silu_gate = gate_pre * sigmoid_gate
    hidden = after((silu_gate * up_pre).astype(BF16), down_parts)
    for held, order in zip(down_parts, (order_a, order_b)):
        for bit in order[1:]:
            net.grow(held, bit)
    down_pieces = [
        (start, span, net.pairs, [held[m] for m in range(net.pairs)])
        for held, (start, span, _) in zip(down_parts, colours)
    ]
    grad_down = down_grad(net, cotangent_both.T, hidden, colours)
    fold_down = [Fold(net, g, order) for g, (_, _, order) in zip(grad_down, colours)]
    launch_all(fold_down)
    down_half = assemble(
        net, down_pieces, width, pair_index, units // 4, 4, lambda i, p: i
    )
    d_hidden = contract(after(cotangent_both, grad_down), down_half, 1, 1)
    d_gate = (d_hidden * up_pre * sigmoid_gate * (1.0 + gate_pre * (1.0 - sigmoid_gate))).astype(
        BF16
    )
    d_up = (d_hidden * silu_gate).astype(BF16)
    normed_both_t = normed_both.T

    def sum_pairs(grad):
        return lax.psum_scatter(
            grad, "rep", scatter_dimension=0, tiled=True, axis_index_groups=net.same_half
        )[0]

    d_gate, d_up = after((d_gate, d_up), got_of(fold_down))
    for fold in fold_down:
        fold.until_last()
    grad_gate = unit_grad(net, normed_both_t, d_gate)
    gate_sum = sum_pairs(grad_gate)
    d_gate, d_up = after((d_gate, d_up), grad_gate, got_of(fold_down))
    collect_all(fold_down)
    first = [f.keep[0, :shard_units] for f in fold_down]
    second = [f.keep[0, shard_units:] for f in fold_down]
    mine = [jnp.where(even, u, v) for u, v in zip(first, second)]
    got = [net.flip_seq(jnp.where(even, v, u), 1) for u, v in zip(first, second)]
    grad_up = unit_grad(net, normed_both_t, d_up)
    up_sum = sum_pairs(grad_up)
    d_gate, d_up = after((d_gate, d_up), grad_up, got)
    total = lambda own, other: (own.astype(F32) + other.astype(F32)).astype(BF16)
    mine = [total(u, v) for u, v in zip(mine, got)]

    def start_seq(folds):
        collect_all(folds)
        both = [f.keep[0].reshape(seqs, -1, f.keep.shape[-1]) for f in folds]
        both = jnp.concatenate(both, axis=1)
        far = net.seq >= seqs // 2
        upper, lower = both[seqs // 2 :], both[: seqs // 2]
        return (
            jnp.where(far, upper, lower),
            net.flip_seq(jnp.where(far, lower, upper), seqs // 2),
        )

    def next_seq(own, got):
        sums = total(own, got)
        return (
            jnp.where(even, sums[0], sums[1]),
            net.flip_seq(jnp.where(even, sums[1], sums[0]), 1),
        )

    def settle_units(piece, order):
        pieces = net.spread(piece, order)
        return [v for m in range(net.pairs) for v in (pieces[m], net.flip(pieces[m], 1))]

    d_normed_both = contract(d_gate, gate_half, 1, 1) + contract(d_up, up_half, 1, 1)
    d_normed_two = d_normed_both[:rows] + net.flip(d_normed_both[rows:], 1)
    grad_gain_two = jnp.sum(d_normed_two * unit_two, axis=0)
    d_mixed = cotangent.astype(F32) + norm_back(d_normed_two * gain_two, unit_two, scale_two, 1)

    d_branch = d_mixed.astype(BF16)
    d_attended_t = contract(out_full, d_branch, 1, 1).astype(BF16)
    d_query_t, d_key_t, d_value_t = attend_backward(
        queries_t, d_attended_t.reshape(H, HD, rows), kv[:KVH], kv_t[:KVH], kv[KVH:], runs
    )
    d_key_t, d_value_t = after((d_key_t, d_value_t), gate_sum)
    d_kv = jnp.concatenate(
        [d_key_t.reshape(kv_width, -1), d_value_t.reshape(kv_width, -1)], axis=0
    )
    lead = (SEQ_BLOCKS - 1) * BLK
    d_kv_own = d_kv[:, lead:]
    need = lead
    step = 1
    backs = []
    while need > 0:
        take = min(need, rows)
        backs.append(d_kv[:, need - take : need].astype(BF16))
        need -= take
    backs = lax.optimization_barrier(backs)
    backs = [net.slide(v, -step - 1) for step, v in enumerate(backs)]
    d_kv_own = after(d_kv_own, backs)
    for back in backs:
        take = back.shape[1]
        d_kv_own = d_kv_own + jnp.pad(back.astype(F32), ((0, 0), (rows - take, 0)))
    sum_seq = lambda v: lax.psum_scatter(v, "seq", scatter_dimension=0, tiled=True)
    gate_sum, up_sum = sum_seq(gate_sum), sum_seq(up_sum)
    mine = after(mine, d_kv_own)
    mine = [total(v, net.flip_seq(v, seqs // 2)) for v in mine]
    mine = [jnp.where(own_half, v, net.flip(v, 1)) for v in mine]
    output_both = contract(after(hidden, d_kv_own), down_half, 1, 0)
    output = (mixed + output_both[:rows] + net.flip(output_both[rows:], 1)).astype(BF16)
    d_query_pre_t = rotate(d_query_t * factor, cosine, -sine).reshape(query_width, rows)
    d_key_pre_t = rotate(d_kv_own[:kv_width].reshape(KVH, HD, rows), cosine, -sine)
    d_proj_t = jnp.concatenate(
        [d_query_pre_t, d_key_pre_t.reshape(kv_width, rows), d_kv_own[kv_width:]], axis=0
    ).astype(BF16)
    d_proj = d_proj_t.T
    grad_bias = jnp.sum(d_proj_t.astype(F32), axis=1)
    d_normed_one = contract(d_proj, proj_full, 1, 1)
    grad_gain_one = jnp.sum(d_normed_one * unit_one, axis=0)
    tokens_grad = (d_mixed + norm_back(d_normed_one * gain_one, unit_one, scale_one, 1)).astype(
        BF16
    )

    gate_sums = settle_units(gate_sum, order_a)
    up_sums = settle_units(up_sum, order_b)
    down_sums = [net.spread(v, order) for v, (_, _, order) in zip(mine, colours)]

    def join_units(sums):
        regions = [
            (lambda place, h=h: ((place[0] + h) % 2) * units, units, net.pairs, sums[h::2])
            for h in range(2)
        ]
        return assemble(
            net, regions, 2 * units, pair_index, shard // 4, 4, lambda i, p: i, dtype=F32
        )

    sum_gate = join_units(gate_sums)
    sum_up = join_units(up_sums)
    sum_down = assemble(
        net,
        [(start, span, net.pairs, v) for v, (start, span, _) in zip(down_sums, colours)],
        width,
        pair_index,
        shard_units // 4,
        4,
        lambda i, p: i,
        dtype=F32,
    )

    pieces_of = lambda v: v.reshape(seqs, -1)
    small = jnp.concatenate(
        [
            pieces_of(grad_gain_one),
            pieces_of(grad_bias[:query_width]),
            pieces_of(grad_bias[query_width : query_width + kv_width]),
            pieces_of(grad_bias[query_width + kv_width :]),
            pieces_of(grad_gain_two),
        ],
        axis=1,
    ).astype(BF16)
    pad = pl.cdiv(shard + 1, 64) * 64 - shard
    small = jnp.pad(small, ((0, 0), (0, attn_columns - small.shape[1])))[:, None]
    small = jnp.pad(small, ((0, 0), (0, pad - 1), (0, 0)))
    attn_orders = [(1,) + tuple(2 * b for b in order) for order in net.orders]
    folds = [
        Fold(net, parts, order, 1)
        for parts, order in zip(
            attn_grad(net, normed_one.T, d_proj, attended_t, d_branch, small, attn_orders),
            attn_orders,
        )
    ]
    launch_all(folds)
    for fold in folds:
        fold.until_last()
    attn_own, attn_got = next_seq(*start_seq(folds))
    attn_sums = settle_units(total(attn_own, attn_got), order_b)
    sum_attn = assemble(
        net,
        [(0, attn_columns, net.reps, attn_sums)],
        attn_columns,
        lambda place: place[0],
        (shard + pad) // 4,
        4,
        lambda i, p: i,
        dtype=F32,
    )
    row = sum_attn[shard]
    sum_gain_one, sum_query_bias, sum_key_bias, sum_value_bias, sum_gain_two = [
        row[e - s : e] for s, e in zip(sizes, ends)
    ]
    a, b, c = query_width, query_width + kv_width, query_width + 2 * kv_width
    return (
        output,
        tokens_grad,
        sum_gain_one,
        sum_attn[:shard, :a],
        sum_query_bias,
        sum_attn[:shard, a:b],
        sum_key_bias,
        sum_attn[:shard, b:c],
        sum_value_bias,
        sum_attn[:shard, c:],
        sum_gain_two,
        sum_gate,
        sum_up,
        sum_down,
    )


def solution(mesh):
    both = ("rep", "seq")
    return jax.shard_map(
        on_device,
        mesh=mesh,
        in_specs=(
            P(both, None),
            P(both, None),
            P(both),
            P(both),
            P(both),
            P("seq"),
            P("seq", None),
            P("seq"),
            P("seq", None),
            P("seq"),
            P("seq", None),
            P("seq"),
            P("seq", None),
            P("seq"),
            P("seq", None),
            P("seq", None),
            P("seq", None),
        ),
        out_specs=(
            P(both, None),
            P(both, None),
            P("seq"),
            P("seq", None),
            P("seq"),
            P("seq", None),
            P("seq"),
            P("seq", None),
            P("seq"),
            P("seq", None),
            P("seq"),
            P("seq", None),
            P("seq", None),
            P("seq", None),
        ),
        check_vma=False,
    )
```

```python
import jax
import jax.numpy as jnp
from jax import lax
from jax.experimental import pallas as pl
from jax.experimental.pallas import tpu as pltpu
from jax.sharding import PartitionSpec as P

H = 14
KVH = 2
HD = 64
BLK = 256
SEQ_BLOCKS = 4
LANES = 128

EPS = 1e-06
ROPE_BASE = 1000000.0

F32 = jnp.float32
BF16 = jnp.bfloat16


class Net:
    def __init__(self):
        self.reps = lax.axis_size("rep")
        self.seqs = lax.axis_size("seq")
        self.rep = lax.axis_index("rep").astype(jnp.int32)
        self.seq = lax.axis_index("seq").astype(jnp.int32)
        self.place = jnp.stack([self.rep, self.seq])
        self.pairs = self.reps // 2
        self.half = self.rep % 2
        self.pair = self.rep // 2
        bits = []
        bit = 1
        while bit < self.pairs:
            bits.append(bit)
            bit *= 2
        self.orders = (tuple(bits), tuple(bits[::-1]))
        self.same_half = [[2 * k + c for k in range(self.pairs)] for c in range(2)]

    def flip(self, value, bit):
        return lax.ppermute(value, "rep", [(i, i ^ bit) for i in range(self.reps)])

    def flip_seq(self, value, bit):
        return lax.ppermute(value, "seq", [(i, i ^ bit) for i in range(self.seqs)])

    def slide(self, value, step):
        pairs = [(i, i + step) for i in range(self.seqs) if 0 <= i + step < self.seqs]
        return lax.ppermute(value, "seq", pairs)

    def gather_seq(self, value):
        return lax.all_gather(value, "seq", axis=0, tiled=True)

    def spread(self, piece, order):
        held = {0: piece}
        for bit in order:
            held.update({m ^ bit: self.flip(v, 2 * bit) for m, v in list(held.items())})
        return [held[m] for m in range(self.pairs)]

    def grow(self, held, bit):
        held.update({m ^ bit: self.flip(v, 2 * bit) for m, v in list(held.items())})


class Fold:
    def __init__(self, net, parts, order, scale=2):
        self.net = net
        self.scale = scale
        self.keep, self.send = parts
        self.bits = list(order)

    def launch(self):
        self.got = self.net.flip(self.send, self.scale * self.bits.pop(0))

    def collect(self):
        half = self.keep.shape[0] // 2
        total = lambda own, got: (own.astype(F32) + got.astype(F32)).astype(BF16)
        if half == 0:
            self.keep = total(self.keep, self.got)
            return
        self.send = total(self.keep[half:], self.got[half:])
        self.keep = total(self.keep[:half], self.got[:half])

    def until_last(self):
        while self.bits:
            self.collect()
            self.launch()


def got_of(folds):
    return [f.got for f in folds]


def launch_all(folds):
    for fold in folds:
        fold.launch()


def collect_all(folds):
    for fold in folds:
        fold.collect()


def after(value, *others):
    return lax.optimization_barrier((value, others))[0]


def cut_width(columns, parts):
    return pl.cdiv(columns // LANES, parts) * LANES


def cut_offset(index, columns, parts):
    width = cut_width(columns, parts)
    return jnp.minimum(index * width, columns - width)


def piece_of_rank(rank, order):
    count = len(order)
    piece = 0
    for at, bit in enumerate(order):
        piece = piece | (((rank >> (count - 1 - at)) & 1) * bit)
    return piece


def assemble(net, regions, columns, index, rows, steps, place_of, own=None, dtype=BF16):
    flat = [p for region in regions for p in region[3]]
    skip = 0 if own is None else 1

    def body(place, *refs):
        out = refs[-1]

        def fill():
            at = 0
            for start, span, parts, pieces in regions:
                for m, piece in enumerate(pieces):
                    base = start(place) if callable(start) else start
                    offset = base + cut_offset(index(place) ^ m, span, parts)
                    col = pl.multiple_of(offset, LANES)
                    out[:, pl.ds(col, piece.shape[1])] = refs[at][...].astype(dtype)
                    at += 1

        if own is None:
            fill()
        else:

            @pl.when(pl.program_id(0) == 0)
            def _():
                out[...] = refs[-2][...]

            @pl.when(pl.program_id(0) > 0)
            def _():
                fill()

    in_specs = [
        pl.BlockSpec((rows, p.shape[1]), lambda i, p: (jnp.maximum(i - skip, 0), 0)) for p in flat
    ]
    if own is not None:
        in_specs.append(pl.BlockSpec((rows, columns), lambda i, p: (0, 0)))
        flat = flat + [own]
    return pl.pallas_call(
        body,
        name="assemble",
        out_shape=jax.ShapeDtypeStruct((rows * steps, columns), dtype),
        grid_spec=pltpu.PrefetchScalarGridSpec(
            num_scalar_prefetch=1,
            grid=(steps,),
            in_specs=in_specs,
            out_specs=pl.BlockSpec((rows, columns), lambda i, p: (place_of(i, p), 0)),
        ),
        cost_estimate=pl.CostEstimate(
            flops=0, transcendentals=0, bytes_accessed=4 * rows * steps * columns
        ),
    )(net.place, *flat)


def pieces_call(net, body, name, left, right, shapes):
    half = net.pairs // 2
    out_shape, out_specs = [], []
    for shape in shapes:
        out_shape += [jax.ShapeDtypeStruct((half,) + shape, BF16)] * 2
        out_specs += [
            pl.BlockSpec((1,) + shape, lambda i, p: (jnp.minimum(i, half - 1), 0, 0)),
            pl.BlockSpec((1,) + shape, lambda i, p: (jnp.maximum(i - half, 0), 0, 0)),
        ]

    def whole(place, left_ref, right_ref, *outs):
        step = pl.program_id(0)
        values = body(step, place[0] // 2, left_ref, right_ref)

        @pl.when(step < half)
        def _():
            for k, value in enumerate(values):
                outs[2 * k][0] = value

        @pl.when(step >= half)
        def _():
            for k, value in enumerate(values):
                outs[2 * k + 1][0] = value

    outs = pl.pallas_call(
        whole,
        name=name,
        out_shape=out_shape,
        grid_spec=pltpu.PrefetchScalarGridSpec(
            num_scalar_prefetch=1,
            grid=(net.pairs,),
            in_specs=[
                pl.BlockSpec(left.shape, lambda i, p: (0, 0)),
                pl.BlockSpec(right.shape, lambda i, p: (0, 0)),
            ],
            out_specs=out_specs,
        ),
        cost_estimate=pl.CostEstimate(
            flops=2 * left.shape[0] * left.shape[1] * right.shape[1],
            transcendentals=0,
            bytes_accessed=2 * (left.size + right.size + left.shape[0] * right.shape[1]),
        ),
    )(net.place, left, right)
    return [tuple(outs[2 * k : 2 * k + 2]) for k in range(len(shapes))]


def unit_grad(net, left_t, right):
    total, tokens = left_t.shape
    columns = right.shape[1]
    width = cut_width(columns, net.pairs)
    start = lambda i: cut_offset(i, columns, net.pairs)

    def body(left_ref, right_ref, out_ref):
        at = pl.multiple_of(start(pl.program_id(0)), LANES)
        out_ref[0] = jnp.dot(
            left_ref[...], right_ref[:, pl.ds(at, width)], preferred_element_type=F32
        ).astype(BF16)

    return pl.pallas_call(
        body,
        name="unit_grad",
        out_shape=jax.ShapeDtypeStruct((net.pairs, total, width), BF16),
        grid=(net.pairs,),
        in_specs=[
            pl.BlockSpec((total, tokens), lambda i: (0, 0)),
            pl.BlockSpec((tokens, columns), lambda i: (0, 0)),
        ],
        out_specs=pl.BlockSpec((1, total, width), lambda i: (i, 0, 0)),
        cost_estimate=pl.CostEstimate(
            flops=2 * total * tokens * columns,
            transcendentals=0,
            bytes_accessed=2 * (left_t.size + right.size + total * columns),
        ),
    )(left_t, right)


def down_grad(net, left_t, right, colours):
    widths = [cut_width(span, net.pairs) for _, span, _ in colours]
    columns = right.shape[1]

    def body(step, pair, left_ref, right_ref):
        slabs = []
        for (start, span, order), width in zip(colours, widths):
            piece = pair ^ piece_of_rank(step, order)
            at = pl.multiple_of(start + cut_offset(piece, span, net.pairs), LANES)
            slabs.append(left_ref[pl.ds(at, width), :])
        val = jnp.dot(
            jnp.concatenate(slabs, axis=0), right_ref[...], preferred_element_type=F32
        ).T.astype(BF16)
        values, at = [], 0
        for width in widths:
            values.append(val[:, at : at + width])
            at += width
        return values

    return pieces_call(net, body, "down_grad", left_t, right, [(columns, w) for w in widths])


def attn_grad(net, first_t, first_right, second_t, second_right, extra, orders):
    reps, seqs = net.reps, net.seqs
    rows = first_t.shape[0] // seqs
    pad = extra.shape[1]
    part = (rows + pad) // len(orders)
    split = first_right.shape[1]
    columns = split + second_right.shape[1]
    width = cut_width(columns, reps)
    half = reps // 2

    def body(place, a_ref, b_ref, c_ref, d_ref, e_ref, *refs):
        outs, full = refs[:-1], refs[-1]
        step = pl.program_id(0)

        @pl.when(step == 0)
        def _():
            first = jnp.dot(a_ref[...], b_ref[...], preferred_element_type=F32).astype(BF16)
            second = jnp.dot(c_ref[...], d_ref[...], preferred_element_type=F32).astype(BF16)
            for s in range(seqs):
                full[s, :rows, :split] = first[s * rows : (s + 1) * rows]
                full[s, :rows, split:] = second[s * rows : (s + 1) * rows]
                full[s, rows:, :] = e_ref[s]

        for k, order in enumerate(orders):
            piece = place[0] ^ piece_of_rank(step, order)
            at = pl.multiple_of(cut_offset(piece, columns, reps), LANES)

            @pl.when(step < half)
            def _():
                outs[2 * k][0] = full[:, k * part : (k + 1) * part, pl.ds(at, width)]

            @pl.when(step >= half)
            def _():
                outs[2 * k + 1][0] = full[:, k * part : (k + 1) * part, pl.ds(at, width)]

    shape = (seqs, part, width)
    out_shape, out_specs = [], []
    for _ in orders:
        out_shape += [jax.ShapeDtypeStruct((half,) + shape, BF16)] * 2
        out_specs += [
            pl.BlockSpec((1,) + shape, lambda i, p: (jnp.minimum(i, half - 1), 0, 0, 0)),
            pl.BlockSpec((1,) + shape, lambda i, p: (jnp.maximum(i - half, 0), 0, 0, 0)),
        ]
    args = (first_t, first_right, second_t, second_right)
    outs = pl.pallas_call(
        body,
        name="attn_grad",
        out_shape=out_shape,
        grid_spec=pltpu.PrefetchScalarGridSpec(
            num_scalar_prefetch=1,
            grid=(reps,),
            in_specs=[pl.BlockSpec(v.shape, lambda i, p: (0, 0)) for v in args]
            + [pl.BlockSpec(extra.shape, lambda i, p: (0, 0, 0))],
            out_specs=out_specs,
            scratch_shapes=[pltpu.VMEM((seqs, rows + pad, columns), BF16)],
        ),
        cost_estimate=pl.CostEstimate(
            flops=2 * first_t.size * columns,
            transcendentals=0,
            bytes_accessed=2 * (seqs * (rows + pad) * columns + 4 * first_t.size),
        ),
    )(net.place, *args, extra)
    return [tuple(outs[2 * k : 2 * k + 2]) for k in range(len(orders))]


def attend_forward(queries_t, keys, values_t, runs):
    heads, size, rows = queries_t.shape
    total = keys.shape[1]
    blocks = rows // BLK
    lead = total // BLK - blocks

    def body(runs_ref, q_ref, k_ref, v_ref, o_ref):
        block = pl.program_id(0)
        run = runs_ref[block]
        for n in range(1, SEQ_BLOCKS + 1):

            @pl.when(run == n - 1)
            def _():
                low = pl.multiple_of((block + (lead + 1 - n)) * BLK, BLK)

                def head(h, carry):
                    g = h // (heads // KVH)
                    scores = jnp.dot(
                        k_ref[g, pl.ds(low, n * BLK), :], q_ref[h], preferred_element_type=F32
                    )
                    top = jnp.max(scores, axis=0, keepdims=True)
                    expon = jnp.exp(scores - top)
                    norm = jnp.sum(expon, axis=0, keepdims=True)
                    out = jnp.dot(
                        v_ref[g, :, pl.ds(low, n * BLK)],
                        expon.astype(BF16),
                        preferred_element_type=F32,
                    )
                    o_ref[h] = (out / norm).astype(BF16)
                    return carry

                lax.fori_loop(0, heads, head, 0, unroll=2)

    return pl.pallas_call(
        body,
        name="attend_forward",
        out_shape=jax.ShapeDtypeStruct((heads, size, rows), BF16),
        grid_spec=pltpu.PrefetchScalarGridSpec(
            num_scalar_prefetch=1,
            grid=(blocks,),
            in_specs=[
                pl.BlockSpec((heads, size, BLK), lambda i, r: (0, 0, i)),
                pl.BlockSpec((KVH, total, size), lambda i, r: (0, 0, 0)),
                pl.BlockSpec((KVH, size, total), lambda i, r: (0, 0, 0)),
            ],
            out_specs=pl.BlockSpec((heads, size, BLK), lambda i, r: (0, 0, i)),
        ),
        cost_estimate=pl.CostEstimate(
            flops=32 * heads * rows * total * size,
            transcendentals=heads * rows * total,
            bytes_accessed=8 * heads * rows * size,
        ),
    )(runs, queries_t, keys, values_t)


def attend_backward(queries_t, grads_t, keys, keys_t, values, runs):
    heads, size, rows = queries_t.shape
    total = keys.shape[1]
    blocks = rows // BLK
    lead = total // BLK - blocks

    def body(runs_ref, q_ref, g_ref, k_ref, kt_ref, v_ref, dq_ref, dk_ref, dv_ref, dk_acc, dv_acc):
        block = pl.program_id(0)
        run = runs_ref[block]

        @pl.when(block == 0)
        def _():
            dk_acc[...] = jnp.zeros_like(dk_acc)
            dv_acc[...] = jnp.zeros_like(dv_acc)

        for n in range(1, SEQ_BLOCKS + 1):

            @pl.when(run == n - 1)
            def _():
                low = pl.multiple_of((block + (lead + 1 - n)) * BLK, BLK)
                span = pl.ds(low, n * BLK)

                def head(h, carry):
                    g = h // (heads // KVH)
                    query_t = q_ref[h]
                    grad_t = g_ref[h]
                    scores = jnp.dot(k_ref[g, span, :], query_t, preferred_element_type=F32)
                    d_probs = jnp.dot(v_ref[g, span, :], grad_t, preferred_element_type=F32)
                    top = jnp.max(scores, axis=0, keepdims=True)
                    expon = jnp.exp(scores - top)
                    probs = expon * (1.0 / jnp.sum(expon, axis=0, keepdims=True))
                    delta = jnp.sum(probs * d_probs, axis=0, keepdims=True)
                    d_scores = (probs * (d_probs - delta)).astype(BF16)
                    dq_ref[h] = jnp.dot(kt_ref[g, :, span], d_scores, preferred_element_type=F32)
                    dk_acc[g, span, :] += jnp.dot(
                        d_scores, query_t.T, preferred_element_type=F32
                    )
                    dv_acc[g, span, :] += jnp.dot(
                        probs.astype(BF16), grad_t.T, preferred_element_type=F32
                    )
                    return carry

                lax.fori_loop(0, heads, head, 0)

        @pl.when(block == blocks - 1)
        def _():
            for g in range(KVH):
                dk_ref[g] = dk_acc[g].T
                dv_ref[g] = dv_acc[g].T

    return pl.pallas_call(
        body,
        name="attend_backward",
        out_shape=(
            jax.ShapeDtypeStruct((heads, size, rows), F32),
            jax.ShapeDtypeStruct((KVH, size, total), F32),
            jax.ShapeDtypeStruct((KVH, size, total), F32),
        ),
        grid_spec=pltpu.PrefetchScalarGridSpec(
            num_scalar_prefetch=1,
            grid=(blocks,),
            in_specs=[
                pl.BlockSpec((heads, size, BLK), lambda i, r: (0, 0, i)),
                pl.BlockSpec((heads, size, BLK), lambda i, r: (0, 0, i)),
                pl.BlockSpec((KVH, total, size), lambda i, r: (0, 0, 0)),
                pl.BlockSpec((KVH, size, total), lambda i, r: (0, 0, 0)),
                pl.BlockSpec((KVH, total, size), lambda i, r: (0, 0, 0)),
            ],
            out_specs=(
                pl.BlockSpec((heads, size, BLK), lambda i, r: (0, 0, i)),
                pl.BlockSpec((KVH, size, total), lambda i, r: (0, 0, 0)),
                pl.BlockSpec((KVH, size, total), lambda i, r: (0, 0, 0)),
            ),
            scratch_shapes=[
                pltpu.VMEM((KVH, total, size), F32),
                pltpu.VMEM((KVH, total, size), F32),
            ],
        ),
        cost_estimate=pl.CostEstimate(
            flops=64 * heads * rows * total * size,
            transcendentals=heads * rows * total,
            bytes_accessed=8 * heads * rows * size,
        ),
    )(runs, queries_t, grads_t, keys, keys_t, values)


def contract(left, right, left_dim, right_dim):
    return lax.dot_general(
        left, right, (((left_dim,), (right_dim,)), ((), ())), preferred_element_type=F32
    )


def rotate(values, cosine, sine):
    half = HD // 2
    upper, lower = values[:, :half], values[:, half:]
    return jnp.concatenate(
        [upper * cosine - lower * sine, lower * cosine + upper * sine], axis=1
    )


def rms_unit(values, axis):
    scale = lax.rsqrt(jnp.mean(values * values, axis=axis, keepdims=True) + EPS)
    return (values * scale, scale)


def norm_back(grad, unit, scale, axis):
    return scale * (grad - unit * jnp.mean(grad * unit, axis=axis, keepdims=True))


def on_device(
    tokens,
    cotangent,
    seq_ids,
    block_ids,
    positions,
    first_gain,
    query_weight,
    query_bias,
    key_weight,
    key_bias,
    value_weight,
    value_bias,
    out_weight,
    second_gain,
    gate_weight,
    up_weight,
    down_weight,
):
    net = Net()
    seqs = net.seqs
    order_a, order_b = net.orders
    rows, width = tokens.shape
    kv_width = KVH * HD
    query_width = H * HD
    runs = block_ids[::BLK]
    own_half = net.seq // (seqs // 2) == net.half
    even = net.seq % 2 == 0

    attn_shard = jnp.concatenate([query_weight, key_weight, value_weight, out_weight], axis=1)
    attn_columns = attn_shard.shape[1]
    vectors = jnp.concatenate([first_gain, query_bias, key_bias, value_bias, second_gain])
    sizes = [
        first_gain.shape[0],
        query_bias.shape[0],
        key_bias.shape[0],
        value_bias.shape[0],
        second_gain.shape[0],
    ]
    ends = [sum(sizes[: i + 1]) for i in range(len(sizes))]
    shard = attn_shard.shape[0]
    attn_width = cut_width(attn_columns, net.reps)
    units = gate_weight.shape[1] // 2
    unit_width = cut_width(units, net.pairs)

    def cut_units(weight):
        start = net.half * units + cut_offset(net.pair, units, net.pairs)
        return lax.dynamic_slice_in_dim(weight, start, unit_width, 1)

    unit_pieces = jnp.concatenate([cut_units(gate_weight), cut_units(up_weight)], axis=0)
    attn_piece = lax.dynamic_slice_in_dim(
        attn_shard, cut_offset(net.rep, attn_columns, net.reps), attn_width, 1
    )
    attn_piece = after(attn_piece, unit_pieces)
    extra = pl.cdiv(vectors.shape[0], attn_width * 8) * 8
    vector_rows = jnp.pad(vectors, (0, extra * attn_width - vectors.shape[0])).reshape(
        extra, attn_width
    )
    attn_seq = net.gather_seq(jnp.concatenate([attn_piece, vector_rows], axis=0)).reshape(
        seqs, shard + extra, attn_width
    )
    vector_all = attn_seq[:, shard:].reshape(seqs, -1).astype(F32)
    attn_seq = attn_seq[:, :shard].reshape(seqs * shard, attn_width)
    gain_one, query_bias_f, key_bias_f, value_bias_f, gain_two = [
        vector_all[:, e - s : e].reshape(-1) for s, e in zip(sizes, ends)
    ]
    top, low = attn_seq[: seqs * shard // 2], attn_seq[seqs * shard // 2 :]
    pieces = [net.spread(top, order_a), net.spread(low, order_b)]
    pieces = [
        [v for m in range(net.pairs) for v in (group[m], net.flip(group[m], 1))]
        for group in pieces
    ]
    part = seqs * shard // 2
    attn_full = jnp.concatenate(
        [
            assemble(
                net,
                [(0, attn_columns, net.reps, group)],
                attn_columns,
                lambda place: place[0],
                part // 2,
                2,
                lambda i, p: i,
            )
            for group in pieces
        ],
        axis=0,
    )
    proj_full = attn_full[:, : query_width + 2 * kv_width]
    out_full = attn_full[:, query_width + 2 * kv_width :]

    both_seq = net.gather_seq(unit_pieces).reshape(seqs, 2, shard, unit_width)
    both_seq = jnp.concatenate([both_seq, both_seq], axis=0)
    both_seq = lax.dynamic_slice_in_dim(both_seq, net.seq + 1, seqs - 1, 0)
    gate_seq = both_seq[:, 0].reshape((seqs - 1) * shard, unit_width)
    up_seq = both_seq[:, 1].reshape((seqs - 1) * shard, unit_width)

    shard_units = down_weight.shape[0]
    tiles = width // LANES
    split = pl.cdiv(tiles, 2) * LANES
    colours = [(0, split, order_a), (split, width - split, order_b)]
    down_cuts = [
        lax.dynamic_slice_in_dim(
            down_weight,
            start + cut_offset(net.pair, span, net.pairs),
            cut_width(span, net.pairs),
            1,
        )
        for start, span, _ in colours
    ]

    cotangent_both = jnp.concatenate([cotangent, net.flip(cotangent, 1)], axis=0)

    tokens_wide = tokens.astype(F32)
    unit_one, scale_one = rms_unit(tokens_wide, 1)
    normed_one = (unit_one * gain_one).astype(BF16)
    freqs = ROPE_BASE ** (-(jnp.arange(HD // 2, dtype=F32) * 2.0 / HD))
    angles = freqs[:, None] * positions.astype(F32)[None, :]
    cosine, sine = jnp.cos(angles), jnp.sin(angles)
    bias = jnp.concatenate([query_bias_f, key_bias_f, value_bias_f])
    proj_t = contract(proj_full, normed_one, 0, 1) + bias[:, None]
    factor = HD ** (-0.5)
    queries_t = rotate(proj_t[:query_width].reshape(H, HD, rows), cosine, sine)
    queries_t = (queries_t.astype(BF16).astype(F32) * factor).astype(BF16)
    keys_own = rotate(
        proj_t[query_width : query_width + kv_width].reshape(KVH, HD, rows), cosine, sine
    ).astype(BF16)
    values_own = proj_t[query_width + kv_width :].astype(BF16)
    kv_own = jnp.concatenate([keys_own.reshape(kv_width, rows), values_own], axis=0)
    gate_parts, up_parts = {0: gate_seq}, {0: up_seq}
    bits_a, bits_b = list(order_a), list(order_b)
    net.grow(gate_parts, bits_a[0])
    net.grow(up_parts, bits_b[0])
    halo = []
    need = (SEQ_BLOCKS - 1) * BLK
    step = 1
    while need > 0:
        take = min(need, rows)
        halo.insert(0, net.slide(kv_own[:, rows - take :], step))
        need -= take
        step += 1
    kv_t = jnp.concatenate(halo + [kv_own], axis=1).reshape(2 * KVH, HD, -1)
    kv_t = after(kv_t, gate_parts, up_parts)
    down_cuts = after(down_cuts, kv_t)
    down_got = [net.flip_seq(v, seqs // 2) for v in down_cuts]
    for bit_a, bit_b in zip(bits_a[1:], bits_b[1:]):
        net.grow(gate_parts, bit_a)
        net.grow(up_parts, bit_b)
    gate_pieces = [gate_parts[m] for m in range(net.pairs)]
    up_pieces = [up_parts[m] for m in range(net.pairs)]
    kv = jnp.transpose(kv_t, (0, 2, 1))
    attended_t = attend_forward(queries_t, kv[:KVH], kv_t[KVH:], runs)
    attended_t = after(attended_t.reshape(query_width, rows), down_got)
    held = [jnp.where(own_half, u, v) for u, v in zip(down_cuts, down_got)]
    other = [net.flip_seq(v, 1) for v in held]
    mixed = tokens_wide + contract(attended_t, out_full, 0, 0)

    unit_two, scale_two = rms_unit(mixed, 1)
    normed_two = (unit_two * gain_two).astype(BF16)
    normed_both = jnp.concatenate([normed_two, net.flip(normed_two, 1)], axis=0)
    pair_index = lambda place: place[0] // 2
    next_shard = lambda i, p: (p[1] + i) % seqs

    def assemble_units(pieces, weight):
        own = lax.dynamic_slice_in_dim(weight, net.half * units, units, 1)
        region = (0, units, net.pairs, pieces)
        return assemble(net, [region], units, pair_index, shard, seqs, next_shard, own)

    gate_half = assemble_units(gate_pieces, gate_weight)
    up_half = assemble_units(up_pieces, up_weight)
    gate_pre = contract(normed_both, gate_half, 1, 0)
    down_seq = [
        jnp.concatenate([jnp.where(even, u, v), jnp.where(even, v, u)], axis=0)
        for u, v in zip(held, other)
    ]
    down_parts = [{0: v} for v in down_seq]
    for held, order in zip(down_parts, (order_a, order_b)):
        net.grow(held, order[0])
    up_pre = contract(after(normed_both, other, gate_pre), up_half, 1, 0)
    sigmoid_gate = jax.nn.sigmoid(gate_pre)
    silu_gate = gate_pre * sigmoid_gate
    hidden = after((silu_gate * up_pre).astype(BF16), down_parts)
    for held, order in zip(down_parts, (order_a, order_b)):
        for bit in order[1:]:
            net.grow(held, bit)
    down_pieces = [
        (start, span, net.pairs, [held[m] for m in range(net.pairs)])
        for held, (start, span, _) in zip(down_parts, colours)
    ]
    grad_down = down_grad(net, cotangent_both.T, hidden, colours)
    fold_down = [Fold(net, g, order) for g, (_, _, order) in zip(grad_down, colours)]
    launch_all(fold_down)
    down_half = assemble(
        net, down_pieces, width, pair_index, units // 4, 4, lambda i, p: i
    )
    d_hidden = contract(after(cotangent_both, grad_down), down_half, 1, 1)
    d_gate = (d_hidden * up_pre * sigmoid_gate * (1.0 + gate_pre * (1.0 - sigmoid_gate))).astype(
        BF16
    )
    d_up = (d_hidden * silu_gate).astype(BF16)
    normed_both_t = normed_both.T

    def sum_pairs(grad):
        return lax.psum_scatter(
            grad, "rep", scatter_dimension=0, tiled=True, axis_index_groups=net.same_half
        )[0]

    d_gate, d_up = after((d_gate, d_up), got_of(fold_down))
    for fold in fold_down:
        fold.until_last()
    grad_gate = unit_grad(net, normed_both_t, d_gate)
    gate_sum = sum_pairs(grad_gate)
    d_gate, d_up = after((d_gate, d_up), grad_gate)
    grad_up = unit_grad(net, normed_both_t, d_up)
    up_sum = sum_pairs(grad_up)
    d_gate, d_up = after((d_gate, d_up), grad_up, got_of(fold_down))
    collect_all(fold_down)
    first = [f.keep[0, :shard_units] for f in fold_down]
    second = [f.keep[0, shard_units:] for f in fold_down]
    mine = [jnp.where(even, u, v) for u, v in zip(first, second)]
    got = [net.flip_seq(jnp.where(even, v, u), 1) for u, v in zip(first, second)]
    total = lambda own, other: (own.astype(F32) + other.astype(F32)).astype(BF16)

    def start_seq(folds):
        collect_all(folds)
        both = [f.keep[0].reshape(seqs, -1, f.keep.shape[-1]) for f in folds]
        both = jnp.concatenate(both, axis=1)
        far = net.seq >= seqs // 2
        upper, lower = both[seqs // 2 :], both[: seqs // 2]
        return (
            jnp.where(far, upper, lower),
            net.flip_seq(jnp.where(far, lower, upper), seqs // 2),
        )

    def next_seq(own, got):
        sums = total(own, got)
        return (
            jnp.where(even, sums[0], sums[1]),
            net.flip_seq(jnp.where(even, sums[1], sums[0]), 1),
        )

    def settle_units(piece, order):
        pieces = net.spread(piece, order)
        return [v for m in range(net.pairs) for v in (pieces[m], net.flip(pieces[m], 1))]

    d_normed_both = contract(d_gate, gate_half, 1, 1) + contract(d_up, up_half, 1, 1)
    d_normed_both = after(d_normed_both, got)
    mine = [total(u, v) for u, v in zip(mine, got)]
    got = [net.flip_seq(v, seqs // 2) for v in mine]
    d_normed_two = d_normed_both[:rows] + net.flip(d_normed_both[rows:], 1)
    grad_gain_two = jnp.sum(d_normed_two * unit_two, axis=0)
    d_mixed = cotangent.astype(F32) + norm_back(d_normed_two * gain_two, unit_two, scale_two, 1)

    d_branch = d_mixed.astype(BF16)
    d_attended_t = contract(out_full, d_branch, 1, 1).astype(BF16)
    d_query_t, d_key_t, d_value_t = attend_backward(
        queries_t, d_attended_t.reshape(H, HD, rows), kv[:KVH], kv_t[:KVH], kv[KVH:], runs
    )
    d_key_t, d_value_t = after((d_key_t, d_value_t), gate_sum, got)
    mine = [total(u, v) for u, v in zip(mine, got)]
    mine = [jnp.where(own_half, v, net.flip(v, 1)) for v in mine]
    d_kv = jnp.concatenate(
        [d_key_t.reshape(kv_width, -1), d_value_t.reshape(kv_width, -1)], axis=0
    )
    lead = (SEQ_BLOCKS - 1) * BLK
    d_kv_own = d_kv[:, lead:]
    need = lead
    step = 1
    backs = []
    while need > 0:
        take = min(need, rows)
        backs.append(d_kv[:, need - take : need].astype(BF16))
        need -= take
    backs = lax.optimization_barrier(backs)
    backs = [net.slide(v, -step - 1) for step, v in enumerate(backs)]
    d_kv_own = after(d_kv_own, backs)
    for back in backs:
        take = back.shape[1]
        d_kv_own = d_kv_own + jnp.pad(back.astype(F32), ((0, 0), (rows - take, 0)))
    sum_seq = lambda v: lax.psum_scatter(v, "seq", scatter_dimension=0, tiled=True)
    gate_sum, up_sum = sum_seq(gate_sum), sum_seq(up_sum)
    d_query_pre_t = rotate(d_query_t * factor, cosine, -sine).reshape(query_width, rows)
    d_key_pre_t = rotate(d_kv_own[:kv_width].reshape(KVH, HD, rows), cosine, -sine)
    d_proj_t = jnp.concatenate(
        [d_query_pre_t, d_key_pre_t.reshape(kv_width, rows), d_kv_own[kv_width:]], axis=0
    ).astype(BF16)
    d_proj = d_proj_t.T
    grad_bias = jnp.sum(d_proj_t.astype(F32), axis=1)
    d_normed_one = contract(d_proj, proj_full, 1, 1)
    grad_gain_one = jnp.sum(d_normed_one * unit_one, axis=0)
    tokens_grad = (d_mixed + norm_back(d_normed_one * gain_one, unit_one, scale_one, 1)).astype(
        BF16
    )

    gate_sums = settle_units(gate_sum, order_a)
    up_sums = settle_units(up_sum, order_b)
    def join_units(sums):
        regions = [
            (lambda place, h=h: ((place[0] + h) % 2) * units, units, net.pairs, sums[h::2])
            for h in range(2)
        ]
        return assemble(
            net, regions, 2 * units, pair_index, shard // 4, 4, lambda i, p: i, dtype=F32
        )

    pieces_of = lambda v: v.reshape(seqs, -1)
    small = jnp.concatenate(
        [
            pieces_of(grad_gain_one),
            pieces_of(grad_bias[:query_width]),
            pieces_of(grad_bias[query_width : query_width + kv_width]),
            pieces_of(grad_bias[query_width + kv_width :]),
            pieces_of(grad_gain_two),
        ],
        axis=1,
    ).astype(BF16)
    pad = pl.cdiv(shard + 1, 64) * 64 - shard
    small = jnp.pad(small, ((0, 0), (0, attn_columns - small.shape[1])))[:, None]
    small = jnp.pad(small, ((0, 0), (0, pad - 1), (0, 0)))
    attn_orders = [(1,) + tuple(2 * b for b in order) for order in net.orders]
    folds = [
        Fold(net, parts, order, 1)
        for parts, order in zip(
            attn_grad(net, normed_one.T, d_proj, attended_t, d_branch, small, attn_orders),
            attn_orders,
        )
    ]
    launch_all(folds)
    attn_got = got_of(folds)
    mine = after(mine, attn_got)
    for fold in folds:
        fold.until_last()
    output_both = contract(after(hidden, attn_got), down_half, 1, 0)
    output = (mixed + output_both[:rows] + net.flip(output_both[rows:], 1)).astype(BF16)
    attn_own, attn_got = next_seq(*start_seq(folds))
    attn_sums = settle_units(total(attn_own, attn_got), order_b)
    attn_sums = after(attn_sums, gate_sums, up_sums)
    sum_attn = assemble(
        net,
        [(0, attn_columns, net.reps, attn_sums)],
        attn_columns,
        lambda place: place[0],
        (shard + pad) // 4,
        4,
        lambda i, p: i,
        dtype=F32,
    )
    down_sums = [net.spread(v, order) for v, (_, _, order) in zip(mine, colours)]

    down_sums = after(down_sums, gate_sums, up_sums)
    sum_down = assemble(
        net,
        [(start, span, net.pairs, v) for v, (start, span, _) in zip(down_sums, colours)],
        width,
        pair_index,
        shard_units // 4,
        4,
        lambda i, p: i,
        dtype=F32,
    )
    sum_gate = join_units(gate_sums)
    sum_up = join_units(up_sums)
    row = sum_attn[shard]
    sum_gain_one, sum_query_bias, sum_key_bias, sum_value_bias, sum_gain_two = [
        row[e - s : e] for s, e in zip(sizes, ends)
    ]
    a, b, c = query_width, query_width + kv_width, query_width + 2 * kv_width
    return (
        output,
        tokens_grad,
        sum_gain_one,
        sum_attn[:shard, :a],
        sum_query_bias,
        sum_attn[:shard, a:b],
        sum_key_bias,
        sum_attn[:shard, b:c],
        sum_value_bias,
        sum_attn[:shard, c:],
        sum_gain_two,
        sum_gate,
        sum_up,
        sum_down,
    )


def solution(mesh):
    both = ("rep", "seq")
    return jax.shard_map(
        on_device,
        mesh=mesh,
        in_specs=(
            P(both, None),
            P(both, None),
            P(both),
            P(both),
            P(both),
            P("seq"),
            P("seq", None),
            P("seq"),
            P("seq", None),
            P("seq"),
            P("seq", None),
            P("seq"),
            P("seq", None),
            P("seq"),
            P("seq", None),
            P("seq", None),
            P("seq", None),
        ),
        out_specs=(
            P(both, None),
            P(both, None),
            P("seq"),
            P("seq", None),
            P("seq"),
            P("seq", None),
            P("seq"),
            P("seq", None),
            P("seq"),
            P("seq", None),
            P("seq"),
            P("seq", None),
            P("seq", None),
            P("seq", None),
        ),
        check_vma=False,
    )
```

```python
import jax
import jax.numpy as jnp
from jax import lax
from jax.experimental import pallas as pl
from jax.experimental.pallas import tpu as pltpu
from jax.sharding import PartitionSpec as P

H = 14
KVH = 2
HD = 64
BLK = 256
SEQ_BLOCKS = 4
LANES = 128

EPS = 1e-06
ROPE_BASE = 1000000.0

F32 = jnp.float32
BF16 = jnp.bfloat16


class Net:
    def __init__(self):
        self.reps = lax.axis_size("rep")
        self.seqs = lax.axis_size("seq")
        self.rep = lax.axis_index("rep").astype(jnp.int32)
        self.seq = lax.axis_index("seq").astype(jnp.int32)
        self.place = jnp.stack([self.rep, self.seq])
        self.pairs = self.reps // 2
        self.half = self.rep % 2
        self.pair = self.rep // 2
        bits = []
        bit = 1
        while bit < self.pairs:
            bits.append(bit)
            bit *= 2
        self.orders = (tuple(bits), tuple(bits[::-1]))
        self.same_half = [[2 * k + c for k in range(self.pairs)] for c in range(2)]

    def flip(self, value, bit):
        return lax.ppermute(value, "rep", [(i, i ^ bit) for i in range(self.reps)])

    def flip_seq(self, value, bit):
        return lax.ppermute(value, "seq", [(i, i ^ bit) for i in range(self.seqs)])

    def slide(self, value, step):
        pairs = [(i, i + step) for i in range(self.seqs) if 0 <= i + step < self.seqs]
        return lax.ppermute(value, "seq", pairs)

    def gather_seq(self, value):
        return lax.all_gather(value, "seq", axis=0, tiled=True)

    def spread(self, piece, order):
        held = {0: piece}
        for bit in order:
            held.update({m ^ bit: self.flip(v, 2 * bit) for m, v in list(held.items())})
        return [held[m] for m in range(self.pairs)]

    def grow(self, held, bit):
        held.update({m ^ bit: self.flip(v, 2 * bit) for m, v in list(held.items())})


class Fold:
    def __init__(self, net, parts, order, scale=2):
        self.net = net
        self.scale = scale
        self.keep, self.send = parts
        self.bits = list(order)

    def launch(self):
        self.got = self.net.flip(self.send, self.scale * self.bits.pop(0))

    def collect(self):
        half = self.keep.shape[0] // 2
        total = lambda own, got: (own.astype(F32) + got.astype(F32)).astype(BF16)
        if half == 0:
            self.keep = total(self.keep, self.got)
            return
        self.send = total(self.keep[half:], self.got[half:])
        self.keep = total(self.keep[:half], self.got[:half])

    def until_last(self):
        while self.bits:
            self.collect()
            self.launch()


def got_of(folds):
    return [f.got for f in folds]


def launch_all(folds):
    for fold in folds:
        fold.launch()


def collect_all(folds):
    for fold in folds:
        fold.collect()


def after(value, *others):
    return lax.optimization_barrier((value, others))[0]


def cut_width(columns, parts):
    return pl.cdiv(columns // LANES, parts) * LANES


def cut_offset(index, columns, parts):
    width = cut_width(columns, parts)
    return jnp.minimum(index * width, columns - width)


def piece_of_rank(rank, order):
    count = len(order)
    piece = 0
    for at, bit in enumerate(order):
        piece = piece | (((rank >> (count - 1 - at)) & 1) * bit)
    return piece


def assemble(net, regions, columns, index, rows, steps, place_of, own=None, dtype=BF16):
    flat = [p for region in regions for p in region[3]]
    skip = 0 if own is None else 1

    def body(place, *refs):
        out = refs[-1]

        def fill():
            at = 0
            for start, span, parts, pieces in regions:
                for m, piece in enumerate(pieces):
                    base = start(place) if callable(start) else start
                    offset = base + cut_offset(index(place) ^ m, span, parts)
                    col = pl.multiple_of(offset, LANES)
                    out[:, pl.ds(col, piece.shape[1])] = refs[at][...].astype(dtype)
                    at += 1

        if own is None:
            fill()
        else:

            @pl.when(pl.program_id(0) == 0)
            def _():
                out[...] = refs[-2][...]

            @pl.when(pl.program_id(0) > 0)
            def _():
                fill()

    in_specs = [
        pl.BlockSpec((rows, p.shape[1]), lambda i, p: (jnp.maximum(i - skip, 0), 0)) for p in flat
    ]
    if own is not None:
        in_specs.append(pl.BlockSpec((rows, columns), lambda i, p: (0, 0)))
        flat = flat + [own]
    return pl.pallas_call(
        body,
        name="assemble",
        out_shape=jax.ShapeDtypeStruct((rows * steps, columns), dtype),
        grid_spec=pltpu.PrefetchScalarGridSpec(
            num_scalar_prefetch=1,
            grid=(steps,),
            in_specs=in_specs,
            out_specs=pl.BlockSpec((rows, columns), lambda i, p: (place_of(i, p), 0)),
        ),
        cost_estimate=pl.CostEstimate(
            flops=0, transcendentals=0, bytes_accessed=4 * rows * steps * columns
        ),
    )(net.place, *flat)


def pieces_call(net, body, name, left, right, shapes):
    half = net.pairs // 2
    out_shape, out_specs = [], []
    for shape in shapes:
        out_shape += [jax.ShapeDtypeStruct((half,) + shape, BF16)] * 2
        out_specs += [
            pl.BlockSpec((1,) + shape, lambda i, p: (jnp.minimum(i, half - 1), 0, 0)),
            pl.BlockSpec((1,) + shape, lambda i, p: (jnp.maximum(i - half, 0), 0, 0)),
        ]

    def whole(place, left_ref, right_ref, *outs):
        step = pl.program_id(0)
        values = body(step, place[0] // 2, left_ref, right_ref)

        @pl.when(step < half)
        def _():
            for k, value in enumerate(values):
                outs[2 * k][0] = value

        @pl.when(step >= half)
        def _():
            for k, value in enumerate(values):
                outs[2 * k + 1][0] = value

    outs = pl.pallas_call(
        whole,
        name=name,
        out_shape=out_shape,
        grid_spec=pltpu.PrefetchScalarGridSpec(
            num_scalar_prefetch=1,
            grid=(net.pairs,),
            in_specs=[
                pl.BlockSpec(left.shape, lambda i, p: (0, 0)),
                pl.BlockSpec(right.shape, lambda i, p: (0, 0)),
            ],
            out_specs=out_specs,
        ),
        cost_estimate=pl.CostEstimate(
            flops=2 * left.shape[0] * left.shape[1] * right.shape[1],
            transcendentals=0,
            bytes_accessed=2 * (left.size + right.size + left.shape[0] * right.shape[1]),
        ),
    )(net.place, left, right)
    return [tuple(outs[2 * k : 2 * k + 2]) for k in range(len(shapes))]


def unit_grad(net, left_t, right):
    total, tokens = left_t.shape
    columns = right.shape[1]
    width = cut_width(columns, net.pairs)
    start = lambda i: cut_offset(i, columns, net.pairs)

    def body(left_ref, right_ref, out_ref):
        at = pl.multiple_of(start(pl.program_id(0)), LANES)
        out_ref[0] = jnp.dot(
            left_ref[...], right_ref[:, pl.ds(at, width)], preferred_element_type=F32
        ).astype(BF16)

    return pl.pallas_call(
        body,
        name="unit_grad",
        out_shape=jax.ShapeDtypeStruct((net.pairs, total, width), BF16),
        grid=(net.pairs,),
        in_specs=[
            pl.BlockSpec((total, tokens), lambda i: (0, 0)),
            pl.BlockSpec((tokens, columns), lambda i: (0, 0)),
        ],
        out_specs=pl.BlockSpec((1, total, width), lambda i: (i, 0, 0)),
        cost_estimate=pl.CostEstimate(
            flops=2 * total * tokens * columns,
            transcendentals=0,
            bytes_accessed=2 * (left_t.size + right.size + total * columns),
        ),
    )(left_t, right)


def down_grad(net, left_t, right, colours):
    widths = [cut_width(span, net.pairs) for _, span, _ in colours]
    columns = right.shape[1]

    def body(step, pair, left_ref, right_ref):
        slabs = []
        for (start, span, order), width in zip(colours, widths):
            piece = pair ^ piece_of_rank(step, order)
            at = pl.multiple_of(start + cut_offset(piece, span, net.pairs), LANES)
            slabs.append(left_ref[pl.ds(at, width), :])
        val = jnp.dot(
            jnp.concatenate(slabs, axis=0), right_ref[...], preferred_element_type=F32
        ).T.astype(BF16)
        values, at = [], 0
        for width in widths:
            values.append(val[:, at : at + width])
            at += width
        return values

    return pieces_call(net, body, "down_grad", left_t, right, [(columns, w) for w in widths])


def attn_grad(net, first_t, first_right, second_t, second_right, extra, orders):
    reps, seqs = net.reps, net.seqs
    rows = first_t.shape[0] // seqs
    pad = extra.shape[1]
    part = (rows + pad) // len(orders)
    split = first_right.shape[1]
    columns = split + second_right.shape[1]
    width = cut_width(columns, reps)
    half = reps // 2

    def body(place, a_ref, b_ref, c_ref, d_ref, e_ref, *refs):
        outs, full = refs[:-1], refs[-1]
        step = pl.program_id(0)

        @pl.when(step == 0)
        def _():
            first = jnp.dot(a_ref[...], b_ref[...], preferred_element_type=F32).astype(BF16)
            second = jnp.dot(c_ref[...], d_ref[...], preferred_element_type=F32).astype(BF16)
            for s in range(seqs):
                full[s, :rows, :split] = first[s * rows : (s + 1) * rows]
                full[s, :rows, split:] = second[s * rows : (s + 1) * rows]
                full[s, rows:, :] = e_ref[s]

        for k, order in enumerate(orders):
            piece = place[0] ^ piece_of_rank(step, order)
            at = pl.multiple_of(cut_offset(piece, columns, reps), LANES)

            @pl.when(step < half)
            def _():
                outs[2 * k][0] = full[:, k * part : (k + 1) * part, pl.ds(at, width)]

            @pl.when(step >= half)
            def _():
                outs[2 * k + 1][0] = full[:, k * part : (k + 1) * part, pl.ds(at, width)]

    shape = (seqs, part, width)
    out_shape, out_specs = [], []
    for _ in orders:
        out_shape += [jax.ShapeDtypeStruct((half,) + shape, BF16)] * 2
        out_specs += [
            pl.BlockSpec((1,) + shape, lambda i, p: (jnp.minimum(i, half - 1), 0, 0, 0)),
            pl.BlockSpec((1,) + shape, lambda i, p: (jnp.maximum(i - half, 0), 0, 0, 0)),
        ]
    args = (first_t, first_right, second_t, second_right)
    outs = pl.pallas_call(
        body,
        name="attn_grad",
        out_shape=out_shape,
        grid_spec=pltpu.PrefetchScalarGridSpec(
            num_scalar_prefetch=1,
            grid=(reps,),
            in_specs=[pl.BlockSpec(v.shape, lambda i, p: (0, 0)) for v in args]
            + [pl.BlockSpec(extra.shape, lambda i, p: (0, 0, 0))],
            out_specs=out_specs,
            scratch_shapes=[pltpu.VMEM((seqs, rows + pad, columns), BF16)],
        ),
        cost_estimate=pl.CostEstimate(
            flops=2 * first_t.size * columns,
            transcendentals=0,
            bytes_accessed=2 * (seqs * (rows + pad) * columns + 4 * first_t.size),
        ),
    )(net.place, *args, extra)
    return [tuple(outs[2 * k : 2 * k + 2]) for k in range(len(orders))]


def attend_forward(queries_t, keys, values_t, runs):
    heads, size, rows = queries_t.shape
    total = keys.shape[1]
    blocks = rows // BLK
    lead = total // BLK - blocks

    def body(runs_ref, q_ref, k_ref, v_ref, o_ref):
        block = pl.program_id(0)
        run = runs_ref[block]
        for n in range(1, SEQ_BLOCKS + 1):

            @pl.when(run == n - 1)
            def _():
                low = pl.multiple_of((block + (lead + 1 - n)) * BLK, BLK)

                def head(h, carry):
                    g = h // (heads // KVH)
                    scores = jnp.dot(
                        k_ref[g, pl.ds(low, n * BLK), :], q_ref[h], preferred_element_type=F32
                    )
                    top = jnp.max(scores, axis=0, keepdims=True)
                    expon = jnp.exp(scores - top)
                    norm = jnp.sum(expon, axis=0, keepdims=True)
                    out = jnp.dot(
                        v_ref[g, :, pl.ds(low, n * BLK)],
                        expon.astype(BF16),
                        preferred_element_type=F32,
                    )
                    o_ref[h] = (out / norm).astype(BF16)
                    return carry

                lax.fori_loop(0, heads, head, 0, unroll=2)

    return pl.pallas_call(
        body,
        name="attend_forward",
        out_shape=jax.ShapeDtypeStruct((heads, size, rows), BF16),
        grid_spec=pltpu.PrefetchScalarGridSpec(
            num_scalar_prefetch=1,
            grid=(blocks,),
            in_specs=[
                pl.BlockSpec((heads, size, BLK), lambda i, r: (0, 0, i)),
                pl.BlockSpec((KVH, total, size), lambda i, r: (0, 0, 0)),
                pl.BlockSpec((KVH, size, total), lambda i, r: (0, 0, 0)),
            ],
            out_specs=pl.BlockSpec((heads, size, BLK), lambda i, r: (0, 0, i)),
        ),
        cost_estimate=pl.CostEstimate(
            flops=32 * heads * rows * total * size,
            transcendentals=heads * rows * total,
            bytes_accessed=8 * heads * rows * size,
        ),
    )(runs, queries_t, keys, values_t)


def attend_backward(queries_t, grads_t, keys, keys_t, values, runs):
    heads, size, rows = queries_t.shape
    total = keys.shape[1]
    blocks = rows // BLK
    lead = total // BLK - blocks

    def body(runs_ref, q_ref, g_ref, k_ref, kt_ref, v_ref, dq_ref, dk_ref, dv_ref, dk_acc, dv_acc):
        block = pl.program_id(0)
        run = runs_ref[block]

        @pl.when(block == 0)
        def _():
            dk_acc[...] = jnp.zeros_like(dk_acc)
            dv_acc[...] = jnp.zeros_like(dv_acc)

        for n in range(1, SEQ_BLOCKS + 1):

            @pl.when(run == n - 1)
            def _():
                low = pl.multiple_of((block + (lead + 1 - n)) * BLK, BLK)
                span = pl.ds(low, n * BLK)

                def head(h, carry):
                    g = h // (heads // KVH)
                    query_t = q_ref[h]
                    grad_t = g_ref[h]
                    scores = jnp.dot(k_ref[g, span, :], query_t, preferred_element_type=F32)
                    d_probs = jnp.dot(v_ref[g, span, :], grad_t, preferred_element_type=F32)
                    top = jnp.max(scores, axis=0, keepdims=True)
                    expon = jnp.exp(scores - top)
                    probs = expon * (1.0 / jnp.sum(expon, axis=0, keepdims=True))
                    delta = jnp.sum(probs * d_probs, axis=0, keepdims=True)
                    d_scores = (probs * (d_probs - delta)).astype(BF16)
                    dq_ref[h] = jnp.dot(kt_ref[g, :, span], d_scores, preferred_element_type=F32)
                    dk_acc[g, span, :] += jnp.dot(
                        d_scores, query_t.T, preferred_element_type=F32
                    )
                    dv_acc[g, span, :] += jnp.dot(
                        probs.astype(BF16), grad_t.T, preferred_element_type=F32
                    )
                    return carry

                lax.fori_loop(0, heads, head, 0)

        @pl.when(block == blocks - 1)
        def _():
            for g in range(KVH):
                dk_ref[g] = dk_acc[g].T
                dv_ref[g] = dv_acc[g].T

    return pl.pallas_call(
        body,
        name="attend_backward",
        out_shape=(
            jax.ShapeDtypeStruct((heads, size, rows), F32),
            jax.ShapeDtypeStruct((KVH, size, total), F32),
            jax.ShapeDtypeStruct((KVH, size, total), F32),
        ),
        grid_spec=pltpu.PrefetchScalarGridSpec(
            num_scalar_prefetch=1,
            grid=(blocks,),
            in_specs=[
                pl.BlockSpec((heads, size, BLK), lambda i, r: (0, 0, i)),
                pl.BlockSpec((heads, size, BLK), lambda i, r: (0, 0, i)),
                pl.BlockSpec((KVH, total, size), lambda i, r: (0, 0, 0)),
                pl.BlockSpec((KVH, size, total), lambda i, r: (0, 0, 0)),
                pl.BlockSpec((KVH, total, size), lambda i, r: (0, 0, 0)),
            ],
            out_specs=(
                pl.BlockSpec((heads, size, BLK), lambda i, r: (0, 0, i)),
                pl.BlockSpec((KVH, size, total), lambda i, r: (0, 0, 0)),
                pl.BlockSpec((KVH, size, total), lambda i, r: (0, 0, 0)),
            ),
            scratch_shapes=[
                pltpu.VMEM((KVH, total, size), F32),
                pltpu.VMEM((KVH, total, size), F32),
            ],
        ),
        cost_estimate=pl.CostEstimate(
            flops=64 * heads * rows * total * size,
            transcendentals=heads * rows * total,
            bytes_accessed=8 * heads * rows * size,
        ),
    )(runs, queries_t, grads_t, keys, keys_t, values)


def contract(left, right, left_dim, right_dim):
    return lax.dot_general(
        left, right, (((left_dim,), (right_dim,)), ((), ())), preferred_element_type=F32
    )


def rotate(values, cosine, sine):
    half = HD // 2
    upper, lower = values[:, :half], values[:, half:]
    return jnp.concatenate(
        [upper * cosine - lower * sine, lower * cosine + upper * sine], axis=1
    )


def rms_unit(values, axis):
    scale = lax.rsqrt(jnp.mean(values * values, axis=axis, keepdims=True) + EPS)
    return (values * scale, scale)


def norm_back(grad, unit, scale, axis):
    return scale * (grad - unit * jnp.mean(grad * unit, axis=axis, keepdims=True))


def on_device(
    tokens,
    cotangent,
    seq_ids,
    block_ids,
    positions,
    first_gain,
    query_weight,
    query_bias,
    key_weight,
    key_bias,
    value_weight,
    value_bias,
    out_weight,
    second_gain,
    gate_weight,
    up_weight,
    down_weight,
):
    net = Net()
    seqs = net.seqs
    order_a, order_b = net.orders
    rows, width = tokens.shape
    kv_width = KVH * HD
    query_width = H * HD
    runs = block_ids[::BLK]
    own_half = net.seq // (seqs // 2) == net.half
    even = net.seq % 2 == 0

    attn_shard = jnp.concatenate([query_weight, key_weight, value_weight, out_weight], axis=1)
    attn_columns = attn_shard.shape[1]
    vectors = jnp.concatenate([first_gain, query_bias, key_bias, value_bias, second_gain])
    sizes = [
        first_gain.shape[0],
        query_bias.shape[0],
        key_bias.shape[0],
        value_bias.shape[0],
        second_gain.shape[0],
    ]
    ends = [sum(sizes[: i + 1]) for i in range(len(sizes))]
    shard = attn_shard.shape[0]
    attn_width = cut_width(attn_columns, net.reps)
    units = gate_weight.shape[1] // 2
    unit_width = cut_width(units, net.pairs)

    def cut_units(weight):
        start = net.half * units + cut_offset(net.pair, units, net.pairs)
        return lax.dynamic_slice_in_dim(weight, start, unit_width, 1)

    unit_pieces = jnp.concatenate([cut_units(gate_weight), cut_units(up_weight)], axis=0)
    attn_piece = lax.dynamic_slice_in_dim(
        attn_shard, cut_offset(net.rep, attn_columns, net.reps), attn_width, 1
    )
    attn_piece = after(attn_piece, unit_pieces)
    extra = pl.cdiv(vectors.shape[0], attn_width * 8) * 8
    vector_rows = jnp.pad(vectors, (0, extra * attn_width - vectors.shape[0])).reshape(
        extra, attn_width
    )
    attn_seq = net.gather_seq(jnp.concatenate([attn_piece, vector_rows], axis=0)).reshape(
        seqs, shard + extra, attn_width
    )
    vector_all = attn_seq[:, shard:].reshape(seqs, -1).astype(F32)
    attn_seq = attn_seq[:, :shard].reshape(seqs * shard, attn_width)
    gain_one, query_bias_f, key_bias_f, value_bias_f, gain_two = [
        vector_all[:, e - s : e].reshape(-1) for s, e in zip(sizes, ends)
    ]
    top, low = attn_seq[: seqs * shard // 2], attn_seq[seqs * shard // 2 :]
    pieces = [net.spread(top, order_a), net.spread(low, order_b)]
    pieces = [
        [v for m in range(net.pairs) for v in (group[m], net.flip(group[m], 1))]
        for group in pieces
    ]
    part = seqs * shard // 2
    attn_full = jnp.concatenate(
        [
            assemble(
                net,
                [(0, attn_columns, net.reps, group)],
                attn_columns,
                lambda place: place[0],
                part // 2,
                2,
                lambda i, p: i,
            )
            for group in pieces
        ],
        axis=0,
    )
    proj_full = attn_full[:, : query_width + 2 * kv_width]
    out_full = attn_full[:, query_width + 2 * kv_width :]

    both_seq = net.gather_seq(unit_pieces).reshape(seqs, 2, shard, unit_width)
    both_seq = jnp.concatenate([both_seq, both_seq], axis=0)
    both_seq = lax.dynamic_slice_in_dim(both_seq, net.seq + 1, seqs - 1, 0)
    gate_seq = both_seq[:, 0].reshape((seqs - 1) * shard, unit_width)
    up_seq = both_seq[:, 1].reshape((seqs - 1) * shard, unit_width)

    shard_units = down_weight.shape[0]
    tiles = width // LANES
    split = pl.cdiv(tiles, 2) * LANES
    colours = [(0, split, order_a), (split, width - split, order_b)]
    down_cuts = [
        lax.dynamic_slice_in_dim(
            down_weight,
            start + cut_offset(net.pair, span, net.pairs),
            cut_width(span, net.pairs),
            1,
        )
        for start, span, _ in colours
    ]

    cotangent_both = jnp.concatenate([cotangent, net.flip(cotangent, 1)], axis=0)

    tokens_wide = tokens.astype(F32)
    unit_one, scale_one = rms_unit(tokens_wide, 1)
    normed_one = (unit_one * gain_one).astype(BF16)
    freqs = ROPE_BASE ** (-(jnp.arange(HD // 2, dtype=F32) * 2.0 / HD))
    angles = freqs[:, None] * positions.astype(F32)[None, :]
    cosine, sine = jnp.cos(angles), jnp.sin(angles)
    bias = jnp.concatenate([query_bias_f, key_bias_f, value_bias_f])
    proj_t = contract(proj_full, normed_one, 0, 1) + bias[:, None]
    factor = HD ** (-0.5)
    queries_t = rotate(proj_t[:query_width].reshape(H, HD, rows), cosine, sine)
    queries_t = (queries_t.astype(BF16).astype(F32) * factor).astype(BF16)
    keys_own = rotate(
        proj_t[query_width : query_width + kv_width].reshape(KVH, HD, rows), cosine, sine
    ).astype(BF16)
    values_own = proj_t[query_width + kv_width :].astype(BF16)
    kv_own = jnp.concatenate([keys_own.reshape(kv_width, rows), values_own], axis=0)
    gate_parts, up_parts = {0: gate_seq}, {0: up_seq}
    bits_a, bits_b = list(order_a), list(order_b)
    net.grow(gate_parts, bits_a[0])
    net.grow(up_parts, bits_b[0])
    halo = []
    need = (SEQ_BLOCKS - 1) * BLK
    step = 1
    while need > 0:
        take = min(need, rows)
        halo.insert(0, net.slide(kv_own[:, rows - take :], step))
        need -= take
        step += 1
    kv_t = jnp.concatenate(halo + [kv_own], axis=1).reshape(2 * KVH, HD, -1)
    kv_t = after(kv_t, gate_parts, up_parts)
    down_cuts = after(down_cuts, kv_t)
    down_got = [net.flip_seq(v, seqs // 2) for v in down_cuts]
    for bit_a, bit_b in zip(bits_a[1:], bits_b[1:]):
        net.grow(gate_parts, bit_a)
        net.grow(up_parts, bit_b)
    gate_pieces = [gate_parts[m] for m in range(net.pairs)]
    up_pieces = [up_parts[m] for m in range(net.pairs)]
    kv = jnp.transpose(kv_t, (0, 2, 1))
    attended_t = attend_forward(queries_t, kv[:KVH], kv_t[KVH:], runs)
    attended_t = after(attended_t.reshape(query_width, rows), down_got)
    held = [jnp.where(own_half, u, v) for u, v in zip(down_cuts, down_got)]
    other = [net.flip_seq(v, 1) for v in held]
    mixed = tokens_wide + contract(attended_t, out_full, 0, 0)

    unit_two, scale_two = rms_unit(mixed, 1)
    normed_two = (unit_two * gain_two).astype(BF16)
    normed_both = jnp.concatenate([normed_two, net.flip(normed_two, 1)], axis=0)
    pair_index = lambda place: place[0] // 2
    next_shard = lambda i, p: (p[1] + i) % seqs

    def assemble_units(pieces, weight):
        own = lax.dynamic_slice_in_dim(weight, net.half * units, units, 1)
        region = (0, units, net.pairs, pieces)
        return assemble(net, [region], units, pair_index, shard, seqs, next_shard, own)

    gate_half = assemble_units(gate_pieces, gate_weight)
    up_half = assemble_units(up_pieces, up_weight)
    gate_pre = contract(normed_both, gate_half, 1, 0)
    down_seq = [
        jnp.concatenate([jnp.where(even, u, v), jnp.where(even, v, u)], axis=0)
        for u, v in zip(held, other)
    ]
    down_parts = [{0: v} for v in down_seq]
    for held, order in zip(down_parts, (order_a, order_b)):
        net.grow(held, order[0])
    up_pre = contract(after(normed_both, other, gate_pre), up_half, 1, 0)
    sigmoid_gate = jax.nn.sigmoid(gate_pre)
    silu_gate = gate_pre * sigmoid_gate
    hidden = after((silu_gate * up_pre).astype(BF16), down_parts)
    for held, order in zip(down_parts, (order_a, order_b)):
        for bit in order[1:]:
            net.grow(held, bit)
    down_pieces = [
        (start, span, net.pairs, [held[m] for m in range(net.pairs)])
        for held, (start, span, _) in zip(down_parts, colours)
    ]
    grad_down = down_grad(net, cotangent_both.T, hidden, colours)
    fold_down = [Fold(net, g, order) for g, (_, _, order) in zip(grad_down, colours)]
    launch_all(fold_down)
    down_half = assemble(
        net, down_pieces, width, pair_index, units // 4, 4, lambda i, p: i
    )
    d_hidden = contract(after(cotangent_both, grad_down), down_half, 1, 1)
    d_gate = (d_hidden * up_pre * sigmoid_gate * (1.0 + gate_pre * (1.0 - sigmoid_gate))).astype(
        BF16
    )
    d_up = (d_hidden * silu_gate).astype(BF16)
    normed_both_t = normed_both.T

    def sum_pairs(grad):
        return lax.psum_scatter(
            grad, "rep", scatter_dimension=0, tiled=True, axis_index_groups=net.same_half
        )[0]

    d_gate, d_up = after((d_gate, d_up), got_of(fold_down))
    for fold in fold_down:
        fold.until_last()
    grad_gate = unit_grad(net, normed_both_t, d_gate)
    gate_sum = sum_pairs(grad_gate)
    d_gate, d_up = after((d_gate, d_up), grad_gate)
    grad_up = unit_grad(net, normed_both_t, d_up)
    up_sum = sum_pairs(grad_up)
    d_gate, d_up = after((d_gate, d_up), grad_up, got_of(fold_down))
    collect_all(fold_down)
    first = [f.keep[0, :shard_units] for f in fold_down]
    second = [f.keep[0, shard_units:] for f in fold_down]
    mine = [jnp.where(even, u, v) for u, v in zip(first, second)]
    got = [net.flip_seq(jnp.where(even, v, u), 1) for u, v in zip(first, second)]
    total = lambda own, other: (own.astype(F32) + other.astype(F32)).astype(BF16)

    def start_seq(folds):
        collect_all(folds)
        both = [f.keep[0].reshape(seqs, -1, f.keep.shape[-1]) for f in folds]
        both = jnp.concatenate(both, axis=1)
        far = net.seq >= seqs // 2
        upper, lower = both[seqs // 2 :], both[: seqs // 2]
        return (
            jnp.where(far, upper, lower),
            net.flip_seq(jnp.where(far, lower, upper), seqs // 2),
        )

    def next_seq(own, got):
        sums = total(own, got)
        return (
            jnp.where(even, sums[0], sums[1]),
            net.flip_seq(jnp.where(even, sums[1], sums[0]), 1),
        )

    def settle_units(piece, order):
        pieces = net.spread(piece, order)
        return [v for m in range(net.pairs) for v in (pieces[m], net.flip(pieces[m], 1))]

    d_normed_both = contract(d_gate, gate_half, 1, 1) + contract(d_up, up_half, 1, 1)
    d_normed_both = after(d_normed_both, got)
    mine = [total(u, v) for u, v in zip(mine, got)]
    got = [net.flip_seq(v, seqs // 2) for v in mine]
    d_normed_two = d_normed_both[:rows] + net.flip(d_normed_both[rows:], 1)
    grad_gain_two = jnp.sum(d_normed_two * unit_two, axis=0)
    d_mixed = cotangent.astype(F32) + norm_back(d_normed_two * gain_two, unit_two, scale_two, 1)

    d_branch = d_mixed.astype(BF16)
    d_attended_t = contract(out_full, d_branch, 1, 1).astype(BF16)
    d_query_t, d_key_t, d_value_t = attend_backward(
        queries_t, d_attended_t.reshape(H, HD, rows), kv[:KVH], kv_t[:KVH], kv[KVH:], runs
    )
    d_key_t, d_value_t = after((d_key_t, d_value_t), gate_sum, got)
    mine = [total(u, v) for u, v in zip(mine, got)]
    mine = [jnp.where(own_half, v, net.flip(v, 1)) for v in mine]
    d_kv = jnp.concatenate(
        [d_key_t.reshape(kv_width, -1), d_value_t.reshape(kv_width, -1)], axis=0
    )
    lead = (SEQ_BLOCKS - 1) * BLK
    d_kv_own = d_kv[:, lead:]
    need = lead
    step = 1
    backs = []
    while need > 0:
        take = min(need, rows)
        backs.append(d_kv[:, need - take : need].astype(BF16))
        need -= take
    backs = lax.optimization_barrier(backs)
    backs = [net.slide(v, -step - 1) for step, v in enumerate(backs)]
    d_kv_own = after(d_kv_own, backs)
    for back in backs:
        take = back.shape[1]
        d_kv_own = d_kv_own + jnp.pad(back.astype(F32), ((0, 0), (rows - take, 0)))
    sum_seq = lambda v: lax.psum_scatter(v, "seq", scatter_dimension=0, tiled=True)
    gate_sum, up_sum = sum_seq(gate_sum), sum_seq(up_sum)
    d_query_pre_t = rotate(d_query_t * factor, cosine, -sine).reshape(query_width, rows)
    d_key_pre_t = rotate(d_kv_own[:kv_width].reshape(KVH, HD, rows), cosine, -sine)
    d_proj_t = jnp.concatenate(
        [d_query_pre_t, d_key_pre_t.reshape(kv_width, rows), d_kv_own[kv_width:]], axis=0
    ).astype(BF16)
    d_proj = d_proj_t.T
    grad_bias = jnp.sum(d_proj_t.astype(F32), axis=1)
    d_normed_one = contract(d_proj, proj_full, 1, 1)
    grad_gain_one = jnp.sum(d_normed_one * unit_one, axis=0)
    tokens_grad = (d_mixed + norm_back(d_normed_one * gain_one, unit_one, scale_one, 1)).astype(
        BF16
    )

    gate_sums = settle_units(gate_sum, order_a)
    up_sums = settle_units(up_sum, order_b)
    def join_units(sums):
        regions = [
            (lambda place, h=h: ((place[0] + h) % 2) * units, units, net.pairs, sums[h::2])
            for h in range(2)
        ]
        return assemble(
            net, regions, 2 * units, pair_index, shard // 4, 4, lambda i, p: i, dtype=F32
        )

    pieces_of = lambda v: v.reshape(seqs, -1)
    small = jnp.concatenate(
        [
            pieces_of(grad_gain_one),
            pieces_of(grad_bias[:query_width]),
            pieces_of(grad_bias[query_width : query_width + kv_width]),
            pieces_of(grad_bias[query_width + kv_width :]),
            pieces_of(grad_gain_two),
        ],
        axis=1,
    ).astype(BF16)
    pad = pl.cdiv(shard + 1, 64) * 64 - shard
    small = jnp.pad(small, ((0, 0), (0, attn_columns - small.shape[1])))[:, None]
    small = jnp.pad(small, ((0, 0), (0, pad - 1), (0, 0)))
    attn_orders = [(1,) + tuple(2 * b for b in order) for order in net.orders]
    folds = [
        Fold(net, parts, order, 1)
        for parts, order in zip(
            attn_grad(net, normed_one.T, d_proj, attended_t, d_branch, small, attn_orders),
            attn_orders,
        )
    ]
    launch_all(folds)
    attn_got = got_of(folds)
    mine = after(mine, attn_got)
    for fold in folds:
        fold.until_last()
    output_both = contract(after(hidden, attn_got), down_half, 1, 0)
    output = (mixed + output_both[:rows] + net.flip(output_both[rows:], 1)).astype(BF16)
    attn_own, attn_got = next_seq(*start_seq(folds))
    attn_sums = settle_units(total(attn_own, attn_got), order_b)
    attn_sums = after(attn_sums, gate_sums[::2], up_sums[::2])
    sum_attn = assemble(
        net,
        [(0, attn_columns, net.reps, attn_sums)],
        attn_columns,
        lambda place: place[0],
        (shard + pad) // 4,
        4,
        lambda i, p: i,
        dtype=F32,
    )
    down_sums = [net.spread(v, order) for v, (_, _, order) in zip(mine, colours)]

    down_sums = after(down_sums, gate_sums[::2], up_sums[::2])
    sum_down = assemble(
        net,
        [(start, span, net.pairs, v) for v, (start, span, _) in zip(down_sums, colours)],
        width,
        pair_index,
        shard_units // 4,
        4,
        lambda i, p: i,
        dtype=F32,
    )
    sum_gate = join_units(gate_sums)
    sum_up = join_units(up_sums)
    row = sum_attn[shard]
    sum_gain_one, sum_query_bias, sum_key_bias, sum_value_bias, sum_gain_two = [
        row[e - s : e] for s, e in zip(sizes, ends)
    ]
    a, b, c = query_width, query_width + kv_width, query_width + 2 * kv_width
    return (
        output,
        tokens_grad,
        sum_gain_one,
        sum_attn[:shard, :a],
        sum_query_bias,
        sum_attn[:shard, a:b],
        sum_key_bias,
        sum_attn[:shard, b:c],
        sum_value_bias,
        sum_attn[:shard, c:],
        sum_gain_two,
        sum_gate,
        sum_up,
        sum_down,
    )


def solution(mesh):
    both = ("rep", "seq")
    return jax.shard_map(
        on_device,
        mesh=mesh,
        in_specs=(
            P(both, None),
            P(both, None),
            P(both),
            P(both),
            P(both),
            P("seq"),
            P("seq", None),
            P("seq"),
            P("seq", None),
            P("seq"),
            P("seq", None),
            P("seq"),
            P("seq", None),
            P("seq"),
            P("seq", None),
            P("seq", None),
            P("seq", None),
        ),
        out_specs=(
            P(both, None),
            P(both, None),
            P("seq"),
            P("seq", None),
            P("seq"),
            P("seq", None),
            P("seq"),
            P("seq", None),
            P("seq"),
            P("seq", None),
            P("seq"),
            P("seq", None),
            P("seq", None),
            P("seq", None),
        ),
        check_vma=False,
    )
```
